32 devices in a mesh: section: 8 (over y, x, core), slab: 4 (over z).
Axes of the slice: x: 2, y: 2, z: 4, core: 2. Of those that a mesh axis runs over, the one named last changes fastest.
Arguments:
- fwd_states: bfloat16 [8, 128, 8, 512], P('section', None, 'slab'), may hold values from -6 to 6
- back_states: bfloat16 [8, 128, 8, 512], P('section', None, 'slab'), may hold values from -6 to 6
- back_grads: bfloat16 [8, 128, 8, 512], P('section', None, 'slab'), may hold values from -6 to 6
- batch_in: bfloat16 [128, 8, 512], P(None, 'slab'), may hold values from -6 to 6
- head_state: bfloat16 [128, 8, 512], P(None, 'slab'), may hold values from -6 to 6
- head_grad: bfloat16 [128, 8, 512], P(None, 'slab'), may hold values from -6 to 6
- couplings: bfloat16 [8, 4, 27, 64, 64], P('section'), may hold values from -0.15625 to 0.15625
Outputs:
- fwd_out: bfloat16 [8, 128, 8, 512], P('section', None, 'slab')
- back_in: bfloat16 [8, 128, 8, 512], P('section', None, 'slab')
- back_grad: bfloat16 [8, 128, 8, 512], P('section', None, 'slab')
The draws below stay inside these ranges and needn't reach their ends.
All inputs are finite; a program needn't handle non-finite values.
Results may differ from the reference program's by a relative error of at most 0.006.
Values may be sent and summed in bfloat16 or wider, within the bound.
No kernel may reach another device: no remote copies, remote signals or barrier semaphores. Data moves between devices by JAX's collectives and lax.ppermute only.
A program may use at most 128 MiB of HBM per device.

```python
import jax
import jax.numpy as jnp
from jax import lax

HALF = 64
HGT = 16
WID = 32
PAIRS = 2
DEPTH = 8
SECTIONS = 8
N_SECTION = 8


def shard_levels(own_key, shape, cuts, low, top_value):
    factor_of, own = 1.0, jax.random.fold_in(own_key, 6)
    for dim, parts in cuts:
        heights = jnp.exp(jax.random.uniform(jax.random.fold_in(own, dim), (parts,), jnp.float32, low / len(cuts), top_value / len(cuts)))
        factor_of = factor_of * jnp.repeat(heights, shape[dim] // parts).reshape([-1 if axis == dim else 1 for axis in range(len(shape))])
    return factor_of


def noise(stream_key, shape, scale, reach, pieces=(), kind=jnp.bfloat16):
    factor_of = shard_levels(stream_key, shape, pieces, -0.22, 0.18) if pieces else 1.0
    values = jax.random.normal(stream_key, shape, jnp.float32) * scale * factor_of
    return jnp.minimum(jnp.maximum(values, -reach), reach).astype(kind)


def setup_inputs(seed: int = 0) -> dict:
    arg_keys = jax.random.split(jax.random.key(seed), 8)
    fwd_states = noise(arg_keys[0], (SECTIONS, 2 * HALF, DEPTH, HGT * WID), 1.0, 6.0, ((0, 8), (2, 4)))
    back_states = noise(arg_keys[1], (SECTIONS, 2 * HALF, DEPTH, HGT * WID), 1.0, 6.0, ((0, 8), (2, 4)))
    back_grads = noise(arg_keys[2], (SECTIONS, 2 * HALF, DEPTH, HGT * WID), 1.0, 6.0, ((0, 8), (2, 4)))
    batch_in = noise(arg_keys[3], (2 * HALF, DEPTH, HGT * WID), 1.0, 6.0, ((1, 4),))
    head_state = noise(arg_keys[4], (2 * HALF, DEPTH, HGT * WID), 1.0, 6.0, ((1, 4),))
    head_grad = noise(arg_keys[5], (2 * HALF, DEPTH, HGT * WID), 1.0, 6.0, ((1, 4),))
    couplings = noise(arg_keys[6], (SECTIONS, 2 * PAIRS, 27, HALF, HALF), (27 * HALF) ** -0.5, 0.15625, ((0, 8),))
    return {"fwd_states": fwd_states, "back_states": back_states, "back_grads": back_grads, "batch_in": batch_in, "head_state": head_state, "head_grad": head_grad, "couplings": couplings}


def conv_ref(field, kernels):
    chans = field.shape[0]
    outs = kernels.shape[1]
    lhs = field.astype(jnp.float32).reshape(1, chans, field.shape[1], HGT, WID)
    kern = kernels.astype(jnp.float32).reshape(3, 3, 3, outs, chans).transpose(3, 4, 0, 1, 2)
    result = lax.conv_general_dilated(lhs, kern, (1, 1, 1), ((1, 1), (1, 1), (1, 1)), dimension_numbers=("NCDHW", "OIDHW", "NCDHW"), precision=lax.Precision.HIGHEST)
    return result[0].reshape(outs, field.shape[1], HGT * WID)


def flipped(kernels):
    return jnp.swapaxes(jnp.flip(kernels, 0), 1, 2)


def slope(z):
    sig = jax.nn.sigmoid(z)
    return sig * (1.0 + z * (1.0 - sig))


def one_section(source, target, target_grad, kernels):
    state = source
    for pair in range(PAIRS):
        first, second = state[:HALF], state[HALF:]
        upper = (first.astype(jnp.float32) + jax.nn.silu(conv_ref(second, kernels[2 * pair]))).astype(jnp.bfloat16)
        lower = (second.astype(jnp.float32) + jax.nn.silu(conv_ref(upper, kernels[2 * pair + 1]))).astype(jnp.bfloat16)
        state = jnp.concatenate([upper, lower], 0)
    ystate = target
    grads = target_grad.astype(jnp.float32)
    for pair in range(PAIRS - 1, -1, -1):
        upper, lower = ystate[:HALF], ystate[HALF:]
        grad_up, grad_low = grads[:HALF], grads[HALF:]
        zeta_g = conv_ref(upper, kernels[2 * pair + 1])
        second = (lower.astype(jnp.float32) - jax.nn.silu(zeta_g)).astype(jnp.bfloat16)
        zeta_f = conv_ref(second, kernels[2 * pair])
        first = (upper.astype(jnp.float32) - jax.nn.silu(zeta_f)).astype(jnp.bfloat16)
        inner_u = (slope(zeta_g) * grad_low).astype(jnp.bfloat16)
        carry_up = grad_up + conv_ref(inner_u, flipped(kernels[2 * pair + 1]))
        inner_w = (slope(zeta_f) * carry_up).astype(jnp.bfloat16)
        carry_low = grad_low + conv_ref(inner_w, flipped(kernels[2 * pair]))
        ystate = jnp.concatenate([first, second], 0)
        grads = jnp.concatenate([carry_up, carry_low], 0)
    return state, ystate, grads.astype(jnp.bfloat16)


def reference(fwd_states, back_states, back_grads, batch_in, head_state, head_grad, couplings):
    def per_section(index):
        prior = fwd_states[jnp.maximum(index - 1, 0)]
        source = jnp.where(index == 0, batch_in, prior)
        later = jnp.minimum(index + 1, N_SECTION - 1)
        target = jnp.where(index == N_SECTION - 1, head_state, back_states[later])
        target_grad = jnp.where(index == N_SECTION - 1, head_grad, back_grads[later])
        return one_section(source, target, target_grad, couplings[index])

    return lax.map(per_section, jnp.arange(N_SECTION, dtype=jnp.int32))
```

```python
import functools

import jax
import jax.numpy as jnp
from jax import lax
from jax.experimental import pallas as pl
from jax.experimental.pallas import tpu as pltpu
from jax.sharding import PartitionSpec as P

WID = 32
PAIRS = 2
LANES = 128
F32 = jnp.float32
BF16 = jnp.bfloat16


def dot(a, b):
    return jnp.dot(a, b, preferred_element_type=F32)


def slab_place():
    z = lax.axis_index("slab")
    return z > 0, z < lax.axis_size("slab") - 1


def is_odd():
    return lax.rem(lax.axis_index("section"), 2) == 1


def pick(flag, yes, no):
    return jnp.where(jnp.full(no.shape, flag), yes, no)


def keep(flag, value):
    return jnp.where(jnp.full(value.shape, flag), value, jnp.zeros((), value.dtype))


def prepare(kernels_ref, *out_refs):
    count = 2 * PAIRS
    taps, half = kernels_ref.shape[2], kernels_ref.shape[3]
    row = lax.broadcasted_iota(jnp.int32, (half, half), 0)
    col = lax.broadcasted_iota(jnp.int32, (half, half), 1)
    unit = jnp.where(row == col, 1.0, 0.0).astype(BF16)
    for q in range(count):
        mine = [kernels_ref[0, q, k] for k in range(taps)]
        turned = [
            lax.dot_general(unit, m, (((1,), (1,)), ((), ())), preferred_element_type=F32).astype(BF16)
            for m in mine
        ]
        for b in range(3):
            pieces = [mine[9 * a + 3 * b + c] for a in range(3) for c in range(3)]
            out_refs[q][b * half : (b + 1) * half, :] = jnp.concatenate(pieces, axis=1)
            pieces = [turned[26 - (9 * a + 3 * b + c)] for a in range(3) for c in range(3)]
            out_refs[count + q][b * half : (b + 1) * half, :] = jnp.concatenate(pieces, axis=1)


def shuffle(tiles, planes, chans, back):
    size = tiles * planes * chans
    row = lax.broadcasted_iota(jnp.int32, (size, size), 1 if back else 0)
    col = lax.broadcasted_iota(jnp.int32, (size, size), 0 if back else 1)
    tp, c = row // chans, row % chans
    tile, plane = tp // planes, tp % planes
    return jnp.where(col == c * (tiles * planes) + tile * planes + plane, 1.0, 0.0).astype(BF16)


def chunk_sizes(planes, cells):
    tiles = cells // LANES
    return tiles, 256 // (tiles * planes)


def split_planes(raw, half, planes, cells):
    tiles, chans = chunk_sizes(planes, cells)
    rows = tiles * planes * chans
    matrix = shuffle(tiles, planes, chans, False)
    chunks = raw.shape[0] // rows
    parts = {}
    for g in range(0, chunks, 2):
        both = jnp.concatenate([raw[g * rows : (g + 1) * rows], raw[(g + 1) * rows : (g + 2) * rows]], axis=1)
        got = dot(matrix, both).astype(BF16)
        for i in range(2):
            for p in range(planes):
                pieces = [
                    got[(t * planes + p) * chans : (t * planes + p + 1) * chans, i * LANES : (i + 1) * LANES]
                    for t in range(tiles)
                ]
                parts[g + i, p] = jnp.concatenate(pieces, axis=1)
    per = half // chans
    count = chunks // per
    return [
        [jnp.concatenate([parts[h * per + j, p] for j in range(per)], axis=0) for p in range(planes)]
        for h in range(count)
    ]


def join_planes(values, out_ref, base):
    planes, (half, cells) = len(values), values[0].shape
    tiles, chans = chunk_sizes(planes, cells)
    rows = tiles * planes * chans
    matrix = shuffle(tiles, planes, chans, True)
    for g in range(0, half // chans, 2):
        sides = []
        for i in range(2):
            lines = slice((g + i) * chans, (g + i + 1) * chans)
            sides.append(
                jnp.concatenate(
                    [
                        values[p][lines, t * LANES : (t + 1) * LANES]
                        for t in range(tiles)
                        for p in range(planes)
                    ],
                    axis=0,
                )
            )
        got = dot(matrix, jnp.concatenate(sides, axis=1)).astype(BF16)
        for i in range(2):
            start = base + (g + i) * rows
            out_ref[start : start + rows, :] = got[:, i * LANES : (i + 1) * LANES]


def lay(stack_ref, slot, plane):
    half, cells = plane.shape
    base = slot * 3 * half
    wide = plane.astype(F32)
    column = lax.broadcasted_iota(jnp.int32, wide.shape, 1) % WID
    left = jnp.where(column > 0, pltpu.roll(wide, 1, 1), 0.0)
    right = jnp.where(column < WID - 1, pltpu.roll(wide, cells - 1, 1), 0.0)
    stack_ref[base : base + half, :] = left.astype(BF16)
    stack_ref[base + half : base + 2 * half, :] = plane.astype(BF16)
    stack_ref[base + 2 * half : base + 3 * half, :] = right.astype(BF16)


def conv(stack_ref, slot, weight_ref):
    half = weight_ref.shape[0] // 3
    cells = stack_ref.shape[1]
    begin = (slot - 1) * 3 * half
    total = dot(weight_ref[...], stack_ref[begin : begin + 9 * half, :])
    cell = lax.broadcasted_iota(jnp.int32, (half, cells), 1)
    above = jnp.where(cell >= WID, pltpu.roll(total[:half], WID, 1), 0.0)
    below = jnp.where(cell < cells - WID, pltpu.roll(total[2 * half :], cells - WID, 1), 0.0)
    return above + total[half : 2 * half] + below


def sigmoid(z):
    return jax.nn.sigmoid(z)


def rows_of(ref, index, half):
    return ref[index * half : (index + 1) * half, :]


def unpack_state(edge, wide_half, half, planes, cells, got_ref, edge_ref, own_ref, up_ref, down_ref):
    at = lax.axis_index("section")
    last = lax.axis_size("section") - 1
    at_edge = at == (last if edge else 0)
    raw = pick(at_edge, edge_ref[...], got_ref[...])
    parts = split_planes(raw, half, planes, cells)
    for h in range(2):
        for p in range(planes):
            own_ref[(h * planes + p) * half : (h * planes + p + 1) * half, :] = parts[h][p]
    other = parts[1 - wide_half]
    odd = is_odd()
    base = 0
    if wide_half is not None:
        for p in range(planes):
            up_ref[p * half : (p + 1) * half, :] = parts[wide_half][p]
            down_ref[p * half : (p + 1) * half, :] = parts[wide_half][p]
        base = planes * half
    up_ref[base : base + half, :] = pick(odd, other[0], other[planes - 1])
    down_ref[base : base + half, :] = pick(odd, other[planes - 1], other[0])


def unpack_grad(half, planes, cells, got_ref, edge_ref, own_ref, up_ref, down_ref):
    at_edge = lax.axis_index("section") == lax.axis_size("section") - 1
    raw = pick(at_edge, edge_ref[...], got_ref[...])
    parts = split_planes(raw, half, planes, cells)
    for h in range(2):
        for p in range(planes):
            own_ref[(h * planes + p) * half : (h * planes + p + 1) * half, :] = parts[h][p]
    odd = is_odd()
    up_ref[...] = pick(odd, parts[1][0], parts[1][planes - 1])
    down_ref[...] = pick(odd, parts[1][planes - 1], parts[1][0])


def halos(up_ref, down_ref, index, half):
    has_low, has_high = slab_place()
    odd = is_odd()
    first, second = rows_of(up_ref, index, half), rows_of(down_ref, index, half)
    low = keep(has_low, pick(odd, second, first))
    high = keep(has_high, pick(odd, first, second))
    return low, high


def forward_first(half, planes, own_ref, up_ref, down_ref, f_ref, g_ref, mid_ref, send_ref, s0, s1):
    has_low, has_high = slab_place()
    for p in range(planes):
        low, high = halos(up_ref, down_ref, p, half)
        lay(s0, p, low)
        lay(s0, 2 * planes + p, high)
        lay(s0, planes + p, rows_of(own_ref, planes + p, half))
    low, high = halos(up_ref, down_ref, planes, half)
    firsts = [low] + [rows_of(own_ref, p, half) for p in range(planes)] + [high]
    for j in range(planes + 2):
        z = conv(s0, planes - 1 + j, f_ref)
        y = (firsts[j].astype(F32) + z * sigmoid(z)).astype(BF16)
        if j == 0:
            y = keep(has_low, y)
        if j == planes + 1:
            y = keep(has_high, y)
        mid_ref[j * half : (j + 1) * half, :] = y
        lay(s1, j, y)
    for p in range(planes):
        z = conv(s1, 1 + p, g_ref)
        y = (rows_of(own_ref, planes + p, half).astype(F32) + z * sigmoid(z)).astype(BF16)
        send_ref[p * half : (p + 1) * half, :] = y


def forward_second(half, planes, mid_ref, own_ref, up_ref, down_ref, f_ref, g_ref, out_ref, s0, s1):
    has_low, has_high = slab_place()
    for p in range(planes):
        low, high = halos(up_ref, down_ref, p, half)
        lay(s0, p, low)
        lay(s0, 2 * planes + p, high)
        lay(s0, planes + p, rows_of(own_ref, p, half))
    tops = []
    for j in range(planes + 2):
        z = conv(s0, planes - 1 + j, f_ref)
        y = (rows_of(mid_ref, j, half).astype(F32) + z * sigmoid(z)).astype(BF16)
        if j == 0:
            y = keep(has_low, y)
        elif j == planes + 1:
            y = keep(has_high, y)
        else:
            tops.append(y)
        lay(s1, j, y)
    bottoms = []
    for p in range(planes):
        z = conv(s1, 1 + p, g_ref)
        bottoms.append((rows_of(own_ref, p, half).astype(F32) + z * sigmoid(z)).astype(BF16))
    join_planes(tops, out_ref, 0)
    join_planes(bottoms, out_ref, out_ref.shape[0] // 2)


def turn(z, low_value, grad):
    sig = sigmoid(z)
    second = (low_value.astype(F32) - z * sig).astype(BF16)
    inner = (sig * (1.0 + z * (1.0 - sig)) * grad).astype(BF16)
    return second, inner


def backward_first(
    half, planes, y_ref, g_ref, yu_ref, yd_ref, gu_ref, gd_ref, wg_ref, wf_ref, tg_ref,
    send_ref, second_ref, low_grad_ref, carry_ref, s0, s1, s2,
):
    has_low, has_high = slab_place()
    for p in range(planes):
        low, high = halos(yu_ref, yd_ref, p, half)
        lay(s0, p, low)
        lay(s0, 2 * planes + p, high)
        lay(s0, planes + p, rows_of(y_ref, p, half))
    low, high = halos(yu_ref, yd_ref, planes, half)
    lowers = [low] + [rows_of(y_ref, planes + p, half) for p in range(planes)] + [high]
    low, high = halos(gu_ref, gd_ref, 0, half)
    grads = [low] + [rows_of(g_ref, planes + p, half) for p in range(planes)] + [high]
    for j in range(planes + 2):
        z = conv(s0, planes - 1 + j, wg_ref)
        second, inner = turn(z, lowers[j], grads[j].astype(F32))
        if j == 0:
            second, inner = keep(has_low, second), keep(has_low, inner)
        if j == planes + 1:
            second, inner = keep(has_high, second), keep(has_high, inner)
        second_ref[j * half : (j + 1) * half, :] = second
        low_grad_ref[j * half : (j + 1) * half, :] = grads[j]
        lay(s1, j, second)
        lay(s2, j, inner)
    for p in range(planes):
        z = conv(s1, 1 + p, wf_ref)
        carry = rows_of(g_ref, p, half).astype(F32) + conv(s2, 1 + p, tg_ref)
        first, inner = turn(z, rows_of(y_ref, p, half), carry)
        carry_ref[p * half : (p + 1) * half, :] = carry
        send_ref[p * half : (p + 1) * half, :] = first
        send_ref[(planes + p) * half : (planes + p + 1) * half, :] = inner


def backward_second(
    half, planes, mine_ref, up_ref, down_ref, second_ref, low_grad_ref, carry_ref,
    tf_ref, wg_ref, wf_ref, tg_ref,
    state_ref, inner_ref, low_ref, top_ref, out_up_ref, out_down_ref, s0, s1, s2, s3,
):
    has_low, has_high = slab_place()
    odd = is_odd()
    for p in range(planes):
        low, high = halos(up_ref, down_ref, p, half)
        lay(s0, p, low)
        lay(s0, 2 * planes + p, high)
        lay(s0, planes + p, rows_of(mine_ref, p, half))
        low, high = halos(up_ref, down_ref, planes + p, half)
        lay(s2, p, low)
        lay(s2, 2 * planes + p, high)
        lay(s2, planes + p, rows_of(mine_ref, planes + p, half))
    for j in range(planes + 2):
        grad = rows_of(low_grad_ref, j, half).astype(F32) + conv(s2, planes - 1 + j, tf_ref)
        z = conv(s0, planes - 1 + j, wg_ref)
        second, inner = turn(z, rows_of(second_ref, j, half), grad)
        if j == 0:
            second, inner = keep(has_low, second), keep(has_low, inner)
        elif j == planes + 1:
            second, inner = keep(has_high, second), keep(has_high, inner)
        else:
            low_ref[(j - 1) * half : j * half, :] = grad
            state_ref[(planes + j - 1) * half : (planes + j) * half, :] = second
        lay(s1, j, second)
        lay(s3, j, inner)
    inners = []
    for p in range(planes):
        z = conv(s1, 1 + p, wf_ref)
        carry = rows_of(carry_ref, p, half) + conv(s3, 1 + p, tg_ref)
        first, inner = turn(z, rows_of(mine_ref, p, half), carry)
        state_ref[p * half : (p + 1) * half, :] = first
        top_ref[p * half : (p + 1) * half, :] = carry.astype(BF16)
        inner_ref[p * half : (p + 1) * half, :] = inner
        inners.append(inner)
    out_up_ref[...] = pick(odd, inners[0], inners[planes - 1])
    out_down_ref[...] = pick(odd, inners[planes - 1], inners[0])


def backward_third(half, planes, inner_ref, up_ref, down_ref, low_ref, top_ref, tf_ref, out_ref, s0):
    low, high = halos(up_ref, down_ref, 0, half)
    lay(s0, 0, low)
    lay(s0, planes + 1, high)
    for p in range(planes):
        lay(s0, 1 + p, rows_of(inner_ref, p, half))
    lows = [(rows_of(low_ref, p, half) + conv(s0, 1 + p, tf_ref)).astype(BF16) for p in range(planes)]
    join_planes([rows_of(top_ref, p, half) for p in range(planes)], out_ref, 0)
    join_planes(lows, out_ref, out_ref.shape[0] // 2)


def pack_state(half, planes, state_ref, out_ref):
    for h in range(2):
        join_planes(
            [rows_of(state_ref, h * planes + p, half) for p in range(planes)], out_ref, h * out_ref.shape[0] // 2
        )


def call(body, name, outs, scratch, flops, *args):
    in_place = pl.BlockSpec(memory_space=pltpu.VMEM)
    return pl.pallas_call(
        body,
        name=name,
        out_shape=[jax.ShapeDtypeStruct(shape, dtype) for shape, dtype in outs],
        in_specs=[in_place] * len(args),
        out_specs=[in_place] * len(outs),
        scratch_shapes=[pltpu.VMEM(shape, BF16) for shape in scratch],
        cost_estimate=pl.CostEstimate(flops=flops, bytes_accessed=1 << 20, transcendentals=0),
    )(*args)


def raw_view(block):
    chans, planes, cells = block.shape
    tiles = cells // LANES
    return block.reshape(chans, planes, tiles, LANES).transpose(0, 2, 1, 3).reshape(-1, LANES)


def from_raw(raw, chans, planes, cells):
    tiles = cells // LANES
    return raw.reshape(chans, tiles, planes, LANES).transpose(0, 2, 1, 3).reshape(1, chans, planes, cells)


def round_trips(sections, slabs):
    ahead = []
    for s in range(0, sections, 2):
        order = [s * slabs + z for z in range(slabs)] + [(s + 1) * slabs + z for z in reversed(range(slabs))]
        ahead += list(zip(order, order[1:] + order[:1]))
    return ahead, [(b, a) for a, b in ahead]


def shards(fwd_states, back_states, back_grads, batch_in, head_state, head_grad, couplings):
    sections, slabs = lax.axis_size("section"), lax.axis_size("slab")
    ahead, behind = round_trips(sections, slabs)
    _, chans, planes, cells = fwd_states.shape
    half = chans // 2

    def swap(up, down):
        return lax.ppermute(up, ("section", "slab"), ahead), lax.ppermute(down, ("section", "slab"), behind)

    def along(value, step):
        return lax.ppermute(value, "section", [(s, (s + step) % sections) for s in range(sections)])

    got_y = along(raw_view(back_states[0]), -1)
    got_g = along(raw_view(back_grads[0]), -1)
    got_x = along(raw_view(fwd_states[0]), 1)

    def planes_of(count, dtype=BF16):
        return ((count * half, cells), dtype)

    unit = 2 * 9 * half * 3 * half * cells
    weights = call(
        prepare, "prepare", [((3 * half, 9 * half), BF16)] * (4 * PAIRS), [], unit, couplings
    )
    direct, turned = weights[: 2 * PAIRS], weights[2 * PAIRS :]

    sizes = (half, planes, cells)
    y_own, y_up, y_down = call(
        functools.partial(unpack_state, True, 0, *sizes), "unpack_y",
        [planes_of(2 * planes), planes_of(planes + 1), planes_of(planes + 1)], [], unit, got_y, raw_view(head_state),
    )
    g_own, g_up, g_down = call(
        functools.partial(unpack_grad, *sizes), "unpack_g",
        [planes_of(2 * planes), planes_of(1), planes_of(1)], [], unit, got_g, raw_view(head_grad),
    )
    x_own, x_up, x_down = call(
        functools.partial(unpack_state, False, 1, *sizes), "unpack_x",
        [planes_of(2 * planes), planes_of(planes + 1), planes_of(planes + 1)], [], unit, got_x, raw_view(batch_in),
    )
    yu, yd = swap(y_up, y_down)
    gu, gd = swap(g_up, g_down)
    xu, xd = swap(x_up, x_down)

    wide = ((3 * planes) * 3 * half, cells)
    near = ((planes + 2) * 3 * half, cells)
    send, second, low_grad, carry = call(
        functools.partial(backward_first, half, planes), "backward_first",
        [planes_of(2 * planes), planes_of(planes + 2), planes_of(planes + 2), planes_of(planes, F32)],
        [wide, near, near], 8 * unit,
        y_own, g_own, yu, yd, gu, gd, direct[3], direct[2], turned[3],
    )
    su, sd = swap(send, send)
    mid, low_own = call(
        functools.partial(forward_first, half, planes), "forward_first",
        [planes_of(planes + 2), planes_of(planes)], [wide, near], 6 * unit,
        x_own, xu, xd, direct[0], direct[1],
    )
    fu, fd = swap(low_own, low_own)
    state, inner, low, top, iu, id_ = call(
        functools.partial(backward_second, half, planes), "backward_second",
        [planes_of(2 * planes), planes_of(planes), planes_of(planes, F32), planes_of(planes), planes_of(1), planes_of(1)],
        [wide, near, wide, near], 12 * unit,
        send, su, sd, second, low_grad, carry, turned[2], direct[1], direct[0], turned[1],
    )
    iu, id_ = swap(iu, id_)
    raw_out = ((chans * planes * cells // LANES, LANES), BF16)
    (fwd_raw,) = call(
        functools.partial(forward_second, half, planes), "forward_second", [raw_out], [wide, near], 6 * unit,
        mid, low_own, fu, fd, direct[2], direct[3],
    )
    (state_raw,) = call(functools.partial(pack_state, half, planes), "pack_state", [raw_out], [], unit, state)
    (grad_raw,) = call(
        functools.partial(backward_third, half, planes), "backward_third", [raw_out], [near], 2 * unit,
        inner, iu, id_, low, top, turned[0],
    )
    shape = (chans, planes, cells)
    return from_raw(fwd_raw, *shape), from_raw(state_raw, *shape), from_raw(grad_raw, *shape)


def solution(mesh):
    return jax.shard_map(
        shards,
        mesh=mesh,
        in_specs=(
            P("section", None, "slab", None),
            P("section", None, "slab", None),
            P("section", None, "slab", None),
            P(None, "slab", None),
            P(None, "slab", None),
            P(None, "slab", None),
            P("section", None, None, None, None),
        ),
        out_specs=(
            P("section", None, "slab", None),
            P("section", None, "slab", None),
            P("section", None, "slab", None),
        ),
        check_vma=False,
    )
```

```python
import functools

import jax
import jax.numpy as jnp
from jax import lax
from jax.experimental import pallas as pl
from jax.experimental.pallas import tpu as pltpu
from jax.sharding import PartitionSpec as P

WID = 32
PAIRS = 2
LANES = 128
F32 = jnp.float32
BF16 = jnp.bfloat16


def dot(a, b):
    return jnp.dot(a, b, preferred_element_type=F32)


def slab_place():
    z = lax.axis_index("slab")
    return z > 0, z < lax.axis_size("slab") - 1


def is_odd():
    return lax.rem(lax.axis_index("section"), 2) == 1


def pick(flag, yes, no):
    return jnp.where(jnp.full(no.shape, flag), yes, no)


def keep(flag, value):
    return jnp.where(jnp.full(value.shape, flag), value, jnp.zeros((), value.dtype))


def prepare(kernels_ref, *out_refs):
    count = 2 * PAIRS
    taps, half = kernels_ref.shape[2], kernels_ref.shape[3]
    row = lax.broadcasted_iota(jnp.int32, (half, half), 0)
    col = lax.broadcasted_iota(jnp.int32, (half, half), 1)
    unit = jnp.where(row == col, 1.0, 0.0).astype(BF16)
    for q in range(count):
        mine = [kernels_ref[0, q, k] for k in range(taps)]
        turned = [
            lax.dot_general(unit, m, (((1,), (1,)), ((), ())), preferred_element_type=F32).astype(BF16)
            for m in mine
        ]
        for b in range(3):
            pieces = [mine[9 * a + 3 * b + c] for a in range(3) for c in range(3)]
            out_refs[q][b * half : (b + 1) * half, :] = jnp.concatenate(pieces, axis=1)
            pieces = [turned[26 - (9 * a + 3 * b + c)] for a in range(3) for c in range(3)]
            out_refs[count + q][b * half : (b + 1) * half, :] = jnp.concatenate(pieces, axis=1)


def shuffle(tiles, planes, chans, back):
    size = tiles * planes * chans
    row = lax.broadcasted_iota(jnp.int32, (size, size), 1 if back else 0)
    col = lax.broadcasted_iota(jnp.int32, (size, size), 0 if back else 1)
    tp, c = row // chans, row % chans
    tile, plane = tp // planes, tp % planes
    return jnp.where(col == c * (tiles * planes) + tile * planes + plane, 1.0, 0.0).astype(BF16)


def chunk_sizes(planes, cells):
    tiles = cells // LANES
    return tiles, 256 // (tiles * planes)


def split_planes(raw, half, planes, cells):
    tiles, chans = chunk_sizes(planes, cells)
    rows = tiles * planes * chans
    matrix = shuffle(tiles, planes, chans, False)
    chunks = raw.shape[0] // rows
    parts = {}
    for g in range(0, chunks, 2):
        both = jnp.concatenate([raw[g * rows : (g + 1) * rows], raw[(g + 1) * rows : (g + 2) * rows]], axis=1)
        got = dot(matrix, both).astype(BF16)
        for i in range(2):
            for p in range(planes):
                pieces = [
                    got[(t * planes + p) * chans : (t * planes + p + 1) * chans, i * LANES : (i + 1) * LANES]
                    for t in range(tiles)
                ]
                parts[g + i, p] = jnp.concatenate(pieces, axis=1)
    per = half // chans
    count = chunks // per
    return [
        [jnp.concatenate([parts[h * per + j, p] for j in range(per)], axis=0) for p in range(planes)]
        for h in range(count)
    ]


def join_planes(values, out_ref, base):
    planes, (half, cells) = len(values), values[0].shape
    tiles, chans = chunk_sizes(planes, cells)
    rows = tiles * planes * chans
    matrix = shuffle(tiles, planes, chans, True)
    for g in range(0, half // chans, 2):
        sides = []
        for i in range(2):
            lines = slice((g + i) * chans, (g + i + 1) * chans)
            sides.append(
                jnp.concatenate(
                    [
                        values[p][lines, t * LANES : (t + 1) * LANES]
                        for t in range(tiles)
                        for p in range(planes)
                    ],
                    axis=0,
                )
            )
        got = dot(matrix, jnp.concatenate(sides, axis=1)).astype(BF16)
        for i in range(2):
            start = base + (g + i) * rows
            out_ref[start : start + rows, :] = got[:, i * LANES : (i + 1) * LANES]


def lay(stack_ref, slot, plane):
    half, cells = plane.shape
    base = slot * 3 * half
    wide = plane.astype(F32)
    column = lax.broadcasted_iota(jnp.int32, wide.shape, 1) % WID
    left = jnp.where(column > 0, pltpu.roll(wide, 1, 1), 0.0)
    right = jnp.where(column < WID - 1, pltpu.roll(wide, cells - 1, 1), 0.0)
    stack_ref[base : base + half, :] = left.astype(BF16)
    stack_ref[base + half : base + 2 * half, :] = plane.astype(BF16)
    stack_ref[base + 2 * half : base + 3 * half, :] = right.astype(BF16)


def conv(stack_ref, slot, weight_ref):
    half = weight_ref.shape[0] // 3
    cells = stack_ref.shape[1]
    begin = (slot - 1) * 3 * half
    total = dot(weight_ref[...], stack_ref[begin : begin + 9 * half, :])
    cell = lax.broadcasted_iota(jnp.int32, (half, cells), 1)
    above = jnp.where(cell >= WID, pltpu.roll(total[:half], WID, 1), 0.0)
    below = jnp.where(cell < cells - WID, pltpu.roll(total[2 * half :], cells - WID, 1), 0.0)
    return above + total[half : 2 * half] + below


def sigmoid(z):
    return jax.nn.sigmoid(z)


def rows_of(ref, index, half):
    return ref[index * half : (index + 1) * half, :]


def unpack_state(edge, wide_half, half, planes, cells, got_ref, edge_ref, own_ref, up_ref, down_ref):
    at = lax.axis_index("section")
    last = lax.axis_size("section") - 1
    at_edge = at == (last if edge else 0)
    raw = pick(at_edge, edge_ref[...], got_ref[...])
    parts = split_planes(raw, half, planes, cells)
    for h in range(2):
        for p in range(planes):
            own_ref[(h * planes + p) * half : (h * planes + p + 1) * half, :] = parts[h][p]
    other = parts[1 - wide_half]
    odd = is_odd()
    base = 0
    if wide_half is not None:
        for p in range(planes):
            up_ref[p * half : (p + 1) * half, :] = parts[wide_half][p]
            down_ref[p * half : (p + 1) * half, :] = parts[wide_half][p]
        base = planes * half
    up_ref[base : base + half, :] = pick(odd, other[0], other[planes - 1])
    down_ref[base : base + half, :] = pick(odd, other[planes - 1], other[0])


def unpack_grad(half, planes, cells, got_ref, edge_ref, own_ref, up_ref, down_ref):
    at_edge = lax.axis_index("section") == lax.axis_size("section") - 1
    raw = pick(at_edge, edge_ref[...], got_ref[...])
    parts = split_planes(raw, half, planes, cells)
    for h in range(2):
        for p in range(planes):
            own_ref[(h * planes + p) * half : (h * planes + p + 1) * half, :] = parts[h][p]
    odd = is_odd()
    up_ref[...] = pick(odd, parts[1][0], parts[1][planes - 1])
    down_ref[...] = pick(odd, parts[1][planes - 1], parts[1][0])


def halos(up_ref, down_ref, index, half):
    has_low, has_high = slab_place()
    odd = is_odd()
    first, second = rows_of(up_ref, index, half), rows_of(down_ref, index, half)
    low = keep(has_low, pick(odd, second, first))
    high = keep(has_high, pick(odd, first, second))
    return low, high


def forward_first(half, planes, own_ref, up_ref, down_ref, f_ref, g_ref, mid_ref, send_ref, s0, s1):
    has_low, has_high = slab_place()
    for p in range(planes):
        low, high = halos(up_ref, down_ref, p, half)
        lay(s0, p, low)
        lay(s0, 2 * planes + p, high)
        lay(s0, planes + p, rows_of(own_ref, planes + p, half))
    low, high = halos(up_ref, down_ref, planes, half)
    firsts = [low] + [rows_of(own_ref, p, half) for p in range(planes)] + [high]
    for j in range(planes + 2):
        z = conv(s0, planes - 1 + j, f_ref)
        y = (firsts[j].astype(F32) + z * sigmoid(z)).astype(BF16)
        if j == 0:
            y = keep(has_low, y)
        if j == planes + 1:
            y = keep(has_high, y)
        mid_ref[j * half : (j + 1) * half, :] = y
        lay(s1, j, y)
    for p in range(planes):
        z = conv(s1, 1 + p, g_ref)
        y = (rows_of(own_ref, planes + p, half).astype(F32) + z * sigmoid(z)).astype(BF16)
        send_ref[p * half : (p + 1) * half, :] = y


def forward_second(half, planes, mid_ref, own_ref, up_ref, down_ref, f_ref, g_ref, out_ref, s0, s1):
    has_low, has_high = slab_place()
    for p in range(planes):
        low, high = halos(up_ref, down_ref, p, half)
        lay(s0, p, low)
        lay(s0, 2 * planes + p, high)
        lay(s0, planes + p, rows_of(own_ref, p, half))
    tops = []
    for j in range(planes + 2):
        z = conv(s0, planes - 1 + j, f_ref)
        y = (rows_of(mid_ref, j, half).astype(F32) + z * sigmoid(z)).astype(BF16)
        if j == 0:
            y = keep(has_low, y)
        elif j == planes + 1:
            y = keep(has_high, y)
        else:
            tops.append(y)
        lay(s1, j, y)
    bottoms = []
    for p in range(planes):
        z = conv(s1, 1 + p, g_ref)
        bottoms.append((rows_of(own_ref, p, half).astype(F32) + z * sigmoid(z)).astype(BF16))
    join_planes(tops, out_ref, 0)
    join_planes(bottoms, out_ref, out_ref.shape[0] // 2)


def turn(z, low_value, grad):
    sig = sigmoid(z)
    second = (low_value.astype(F32) - z * sig).astype(BF16)
    inner = (sig * (1.0 + z * (1.0 - sig)) * grad).astype(BF16)
    return second, inner


def backward_first(
    half, planes, y_ref, g_ref, yu_ref, yd_ref, gu_ref, gd_ref, wg_ref, wf_ref, tg_ref,
    send_ref, second_ref, low_grad_ref, carry_ref, s0, s1, s2,
):
    has_low, has_high = slab_place()
    for p in range(planes):
        low, high = halos(yu_ref, yd_ref, p, half)
        lay(s0, p, low)
        lay(s0, 2 * planes + p, high)
        lay(s0, planes + p, rows_of(y_ref, p, half))
    low, high = halos(yu_ref, yd_ref, planes, half)
    lowers = [low] + [rows_of(y_ref, planes + p, half) for p in range(planes)] + [high]
    low, high = halos(gu_ref, gd_ref, 0, half)
    grads = [low] + [rows_of(g_ref, planes + p, half) for p in range(planes)] + [high]
    for j in range(planes + 2):
        z = conv(s0, planes - 1 + j, wg_ref)
        second, inner = turn(z, lowers[j], grads[j].astype(F32))
        if j == 0:
            second, inner = keep(has_low, second), keep(has_low, inner)
        if j == planes + 1:
            second, inner = keep(has_high, second), keep(has_high, inner)
        second_ref[j * half : (j + 1) * half, :] = second
        low_grad_ref[j * half : (j + 1) * half, :] = grads[j]
        lay(s1, j, second)
        lay(s2, j, inner)
    for p in range(planes):
        z = conv(s1, 1 + p, wf_ref)
        carry = rows_of(g_ref, p, half).astype(F32) + conv(s2, 1 + p, tg_ref)
        first, inner = turn(z, rows_of(y_ref, p, half), carry)
        carry_ref[p * half : (p + 1) * half, :] = carry
        send_ref[p * half : (p + 1) * half, :] = first
        send_ref[(planes + p) * half : (planes + p + 1) * half, :] = inner


def backward_second(
    half, planes, mine_ref, up_ref, down_ref, second_ref, low_grad_ref, carry_ref,
    tf_ref, wg_ref, wf_ref, tg_ref,
    state_ref, inner_ref, low_ref, top_ref, out_up_ref, out_down_ref, s0, s1, s2, s3,
):
    has_low, has_high = slab_place()
    odd = is_odd()
    for p in range(planes):
        low, high = halos(up_ref, down_ref, p, half)
        lay(s0, p, low)
        lay(s0, 2 * planes + p, high)
        lay(s0, planes + p, rows_of(mine_ref, p, half))
        low, high = halos(up_ref, down_ref, planes + p, half)
        lay(s2, p, low)
        lay(s2, 2 * planes + p, high)
        lay(s2, planes + p, rows_of(mine_ref, planes + p, half))
    for j in range(planes + 2):
        grad = rows_of(low_grad_ref, j, half).astype(F32) + conv(s2, planes - 1 + j, tf_ref)
        z = conv(s0, planes - 1 + j, wg_ref)
        second, inner = turn(z, rows_of(second_ref, j, half), grad)
        if j == 0:
            second, inner = keep(has_low, second), keep(has_low, inner)
        elif j == planes + 1:
            second, inner = keep(has_high, second), keep(has_high, inner)
        else:
            low_ref[(j - 1) * half : j * half, :] = grad
            state_ref[(planes + j - 1) * half : (planes + j) * half, :] = second
        lay(s1, j, second)
        lay(s3, j, inner)
    inners = []
    for p in range(planes):
        z = conv(s1, 1 + p, wf_ref)
        carry = rows_of(carry_ref, p, half) + conv(s3, 1 + p, tg_ref)
        first, inner = turn(z, rows_of(mine_ref, p, half), carry)
        state_ref[p * half : (p + 1) * half, :] = first
        top_ref[p * half : (p + 1) * half, :] = carry.astype(BF16)
        inner_ref[p * half : (p + 1) * half, :] = inner
        inners.append(inner)
    out_up_ref[...] = pick(odd, inners[0], inners[planes - 1])
    out_down_ref[...] = pick(odd, inners[planes - 1], inners[0])


def backward_third(half, planes, inner_ref, up_ref, down_ref, low_ref, top_ref, tf_ref, out_ref, s0):
    low, high = halos(up_ref, down_ref, 0, half)
    lay(s0, 0, low)
    lay(s0, planes + 1, high)
    for p in range(planes):
        lay(s0, 1 + p, rows_of(inner_ref, p, half))
    lows = [(rows_of(low_ref, p, half) + conv(s0, 1 + p, tf_ref)).astype(BF16) for p in range(planes)]
    join_planes([rows_of(top_ref, p, half) for p in range(planes)], out_ref, 0)
    join_planes(lows, out_ref, out_ref.shape[0] // 2)


def pack_state(half, planes, state_ref, out_ref):
    for h in range(2):
        join_planes(
            [rows_of(state_ref, h * planes + p, half) for p in range(planes)], out_ref, h * out_ref.shape[0] // 2
        )


def call(body, name, outs, scratch, flops, *args):
    in_place = pl.BlockSpec(memory_space=pltpu.VMEM)
    return pl.pallas_call(
        body,
        name=name,
        out_shape=[jax.ShapeDtypeStruct(shape, dtype) for shape, dtype in outs],
        in_specs=[in_place] * len(args),
        out_specs=[in_place] * len(outs),
        scratch_shapes=[pltpu.VMEM(shape, BF16) for shape in scratch],
        compiler_params=pltpu.CompilerParams(vmem_limit_bytes=16 << 20),
        cost_estimate=pl.CostEstimate(flops=flops, bytes_accessed=1 << 20, transcendentals=0),
    )(*args)


def raw_view(block):
    chans, planes, cells = block.shape
    tiles = cells // LANES
    return block.reshape(chans, planes, tiles, LANES).transpose(0, 2, 1, 3).reshape(-1, LANES)


def from_raw(raw, chans, planes, cells):
    tiles = cells // LANES
    return raw.reshape(chans, tiles, planes, LANES).transpose(0, 2, 1, 3).reshape(1, chans, planes, cells)


def round_trips(sections, slabs):
    ahead = []
    for s in range(0, sections, 2):
        order = [s * slabs + z for z in range(slabs)] + [(s + 1) * slabs + z for z in reversed(range(slabs))]
        ahead += list(zip(order, order[1:] + order[:1]))
    return ahead, [(b, a) for a, b in ahead]


def shards(fwd_states, back_states, back_grads, batch_in, head_state, head_grad, couplings):
    sections, slabs = lax.axis_size("section"), lax.axis_size("slab")
    ahead, behind = round_trips(sections, slabs)
    _, chans, planes, cells = fwd_states.shape
    half = chans // 2

    def swap(up, down):
        return lax.ppermute(up, ("section", "slab"), ahead), lax.ppermute(down, ("section", "slab"), behind)

    def along(value, step):
        return lax.ppermute(value, "section", [(s, (s + step) % sections) for s in range(sections)])

    got_y = along(raw_view(back_states[0]), -1)
    got_g = along(raw_view(back_grads[0]), -1)
    got_x = along(raw_view(fwd_states[0]), 1)

    def planes_of(count, dtype=BF16):
        return ((count * half, cells), dtype)

    unit = 2 * 9 * half * 3 * half * cells
    weights = call(
        prepare, "prepare", [((3 * half, 9 * half), BF16)] * (4 * PAIRS), [], unit, couplings
    )
    direct, turned = weights[: 2 * PAIRS], weights[2 * PAIRS :]

    sizes = (half, planes, cells)
    y_own, y_up, y_down = call(
        functools.partial(unpack_state, True, 0, *sizes), "unpack_y",
        [planes_of(2 * planes), planes_of(planes + 1), planes_of(planes + 1)], [], unit, got_y, raw_view(head_state),
    )
    g_own, g_up, g_down = call(
        functools.partial(unpack_grad, *sizes), "unpack_g",
        [planes_of(2 * planes), planes_of(1), planes_of(1)], [], unit, got_g, raw_view(head_grad),
    )
    x_own, x_up, x_down = call(
        functools.partial(unpack_state, False, 1, *sizes), "unpack_x",
        [planes_of(2 * planes), planes_of(planes + 1), planes_of(planes + 1)], [], unit, got_x, raw_view(batch_in),
    )
    yu, yd = swap(y_up, y_down)
    gu, gd = swap(g_up, g_down)
    xu, xd = swap(x_up, x_down)

    wide = ((3 * planes) * 3 * half, cells)
    near = ((planes + 2) * 3 * half, cells)
    send, second, low_grad, carry = call(
        functools.partial(backward_first, half, planes), "backward_first",
        [planes_of(2 * planes), planes_of(planes + 2), planes_of(planes + 2), planes_of(planes, F32)],
        [wide, near, near], 8 * unit,
        y_own, g_own, yu, yd, gu, gd, direct[3], direct[2], turned[3],
    )
    su, sd = swap(send, send)
    mid, low_own = call(
        functools.partial(forward_first, half, planes), "forward_first",
        [planes_of(planes + 2), planes_of(planes)], [wide, near], 6 * unit,
        x_own, xu, xd, direct[0], direct[1],
    )
    fu, fd = swap(low_own, low_own)
    state, inner, low, top, iu, id_ = call(
        functools.partial(backward_second, half, planes), "backward_second",
        [planes_of(2 * planes), planes_of(planes), planes_of(planes, F32), planes_of(planes), planes_of(1), planes_of(1)],
        [wide, near, wide, near], 12 * unit,
        send, su, sd, second, low_grad, carry, turned[2], direct[1], direct[0], turned[1],
    )
    iu, id_ = swap(iu, id_)
    raw_out = ((chans * planes * cells // LANES, LANES), BF16)
    (fwd_raw,) = call(
        functools.partial(forward_second, half, planes), "forward_second", [raw_out], [wide, near], 6 * unit,
        mid, low_own, fu, fd, direct[2], direct[3],
    )
    (state_raw,) = call(functools.partial(pack_state, half, planes), "pack_state", [raw_out], [], unit, state)
    (grad_raw,) = call(
        functools.partial(backward_third, half, planes), "backward_third", [raw_out], [near], 2 * unit,
        inner, iu, id_, low, top, turned[0],
    )
    shape = (chans, planes, cells)
    return from_raw(fwd_raw, *shape), from_raw(state_raw, *shape), from_raw(grad_raw, *shape)


def solution(mesh):
    return jax.shard_map(
        shards,
        mesh=mesh,
        in_specs=(
            P("section", None, "slab", None),
            P("section", None, "slab", None),
            P("section", None, "slab", None),
            P(None, "slab", None),
            P(None, "slab", None),
            P(None, "slab", None),
            P("section", None, None, None, None),
        ),
        out_specs=(
            P("section", None, "slab", None),
            P("section", None, "slab", None),
            P("section", None, "slab", None),
        ),
        check_vma=False,
    )
```

```python
import functools

import jax
import jax.numpy as jnp
from jax import lax
from jax.experimental import pallas as pl
from jax.experimental.pallas import tpu as pltpu
from jax.sharding import PartitionSpec as P


WID = 32
PAIRS = 2
LANES = 128
F32 = jnp.float32
BF16 = jnp.bfloat16


def dot(a, b):
    return jnp.dot(a, b, preferred_element_type=F32)


def slab_place():
    z = lax.axis_index("slab")
    return z > 0, z < lax.axis_size("slab") - 1


def is_odd():
    return lax.rem(lax.axis_index("section"), 2) == 1


def pick(flag, yes, no):
    return jnp.where(jnp.full(no.shape, flag), yes, no)


def keep(flag, value):
    return jnp.where(jnp.full(value.shape, flag), value, jnp.zeros((), value.dtype))


def prepare(planes, cells, kernels_ref, *refs):
    count = 2 * PAIRS
    out_refs, (split_ref, join_ref) = refs[: 2 * count], refs[2 * count :]
    tiles, chans = chunk_sizes(planes, cells)
    split_ref[...] = shuffle(tiles, planes, chans, False)
    join_ref[...] = shuffle(tiles, planes, chans, True)
    taps, half = kernels_ref.shape[2], kernels_ref.shape[3]
    row = lax.broadcasted_iota(jnp.int32, (half, half), 0)
    col = lax.broadcasted_iota(jnp.int32, (half, half), 1)
    unit = jnp.where(row == col, 1.0, 0.0).astype(BF16)
    for q in range(count):
        mine = [kernels_ref[0, q, k] for k in range(taps)]
        turned = [
            lax.dot_general(unit, m, (((1,), (1,)), ((), ())), preferred_element_type=F32).astype(BF16)
            for m in mine
        ]
        blank = jnp.zeros((half, 3 * half), BF16)
        for b in range(3):
            for kind, pieces in (
                (0, [mine[9 * a + 3 * b + c] for a in range(3) for c in range(3)]),
                (count, [turned[26 - (9 * a + 3 * b + c)] for a in range(3) for c in range(3)]),
            ):
                line = jnp.concatenate(pieces, axis=1)
                for j, parts in ((0, [line, blank]), (1, [blank, line])):
                    out_refs[kind + q][(3 * j + b) * half : (3 * j + b + 1) * half, :] = jnp.concatenate(parts, axis=1)


def shuffle(tiles, planes, chans, back):
    size = tiles * planes * chans
    row = lax.broadcasted_iota(jnp.int32, (size, size), 1 if back else 0)
    col = lax.broadcasted_iota(jnp.int32, (size, size), 0 if back else 1)
    tp, c = row // chans, row % chans
    tile, plane = tp // planes, tp % planes
    return jnp.where(col == c * (tiles * planes) + tile * planes + plane, 1.0, 0.0).astype(BF16)


def chunk_sizes(planes, cells):
    tiles = cells // LANES
    return tiles, 256 // (tiles * planes)


def split_planes(raw, matrix, half, planes, cells):
    tiles, chans = chunk_sizes(planes, cells)
    rows = tiles * planes * chans
    chunks = raw.shape[0] // rows
    parts = {}
    for g in range(0, chunks, 2):
        both = jnp.concatenate([raw[g * rows : (g + 1) * rows], raw[(g + 1) * rows : (g + 2) * rows]], axis=1)
        got = dot(matrix, both).astype(BF16)
        for i in range(2):
            for p in range(planes):
                pieces = [
                    got[(t * planes + p) * chans : (t * planes + p + 1) * chans, i * LANES : (i + 1) * LANES]
                    for t in range(tiles)
                ]
                parts[g + i, p] = jnp.concatenate(pieces, axis=1)
    per = half // chans
    count = chunks // per
    return [
        [jnp.concatenate([parts[h * per + j, p] for j in range(per)], axis=0) for p in range(planes)]
        for h in range(count)
    ]


def join_planes(values, matrix, out_ref, base):
    planes, (half, cells) = len(values), values[0].shape
    tiles, chans = chunk_sizes(planes, cells)
    rows = tiles * planes * chans
    for g in range(0, half // chans, 2):
        sides = []
        for i in range(2):
            lines = slice((g + i) * chans, (g + i + 1) * chans)
            sides.append(
                jnp.concatenate(
                    [
                        values[p][lines, t * LANES : (t + 1) * LANES]
                        for t in range(tiles)
                        for p in range(planes)
                    ],
                    axis=0,
                )
            )
        got = dot(matrix, jnp.concatenate(sides, axis=1)).astype(BF16)
        for i in range(2):
            start = base + (g + i) * rows
            out_ref[start : start + rows, :] = got[:, i * LANES : (i + 1) * LANES]


def lay(stack_ref, slot, plane):
    half, cells = plane.shape
    base = slot * 3 * half
    wide = plane.astype(F32)
    column = lax.broadcasted_iota(jnp.int32, wide.shape, 1) % WID
    left = jnp.where(column > 0, pltpu.roll(wide, 1, 1), 0.0)
    right = jnp.where(column < WID - 1, pltpu.roll(wide, cells - 1, 1), 0.0)
    stack_ref[base : base + half, :] = left.astype(BF16)
    stack_ref[base + half : base + 2 * half, :] = plane.astype(BF16)
    stack_ref[base + 2 * half : base + 3 * half, :] = right.astype(BF16)


def conv(stack_ref, slot, weight_ref):
    half = weight_ref.shape[0] // 6
    cells = stack_ref.shape[1]
    begin = (slot - 1) * 3 * half
    total = dot(weight_ref[...], stack_ref[begin : begin + 12 * half, :])
    cell = lax.broadcasted_iota(jnp.int32, (half, cells), 1)
    results = []
    for j in range(2):
        rows = [total[(3 * j + b) * half : (3 * j + b + 1) * half] for b in range(3)]
        above = jnp.where(cell >= WID, pltpu.roll(rows[0], WID, 1), 0.0)
        below = jnp.where(cell < cells - WID, pltpu.roll(rows[2], cells - WID, 1), 0.0)
        results.append(above + rows[1] + below)
    return results


def convs(stack_ref, slot, count, weight_ref):
    for j in range(0, count, 2):
        yield from conv(stack_ref, slot + j, weight_ref)


def sigmoid(z):
    return jax.nn.sigmoid(z)


def rows_of(ref, index, half):
    return ref[index * half : (index + 1) * half, :]


def unpack_state(edge, wide_half, half, planes, cells, got_ref, edge_ref, matrix_ref, own_ref, up_ref, down_ref):
    at = lax.axis_index("section")
    last = lax.axis_size("section") - 1
    at_edge = at == (last if edge else 0)
    raw = pick(at_edge, edge_ref[...], got_ref[...])
    parts = split_planes(raw, matrix_ref[...], half, planes, cells)
    for h in range(2):
        for p in range(planes):
            own_ref[(h * planes + p) * half : (h * planes + p + 1) * half, :] = parts[h][p]
    other = parts[1 - wide_half]
    odd = is_odd()
    base = 0
    if wide_half is not None:
        for p in range(planes):
            up_ref[p * half : (p + 1) * half, :] = parts[wide_half][p]
            down_ref[p * half : (p + 1) * half, :] = parts[wide_half][p]
        base = planes * half
    up_ref[base : base + half, :] = pick(odd, other[0], other[planes - 1])
    down_ref[base : base + half, :] = pick(odd, other[planes - 1], other[0])


def unpack_grad(part, half, planes, cells, got_ref, edge_ref, matrix_ref, own_ref, *send_refs):
    at_edge = lax.axis_index("section") == lax.axis_size("section") - 1
    rows = got_ref.shape[0]
    raw = pick(at_edge, edge_ref[part * rows : (part + 1) * rows, :], got_ref[...])
    (parts,) = split_planes(raw, matrix_ref[...], half, planes, cells)
    for p in range(planes):
        own_ref[p * half : (p + 1) * half, :] = parts[p]
    if send_refs:
        up_ref, down_ref = send_refs
        odd = is_odd()
        up_ref[...] = pick(odd, parts[0], parts[planes - 1])
        down_ref[...] = pick(odd, parts[planes - 1], parts[0])


def halos(up_ref, down_ref, index, half):
    has_low, has_high = slab_place()
    odd = is_odd()
    first, second = rows_of(up_ref, index, half), rows_of(down_ref, index, half)
    low = keep(has_low, pick(odd, second, first))
    high = keep(has_high, pick(odd, first, second))
    return low, high


def forward_first(half, planes, own_ref, up_ref, down_ref, f_ref, g_ref, mid_ref, send_ref, s0, s1):
    has_low, has_high = slab_place()
    for p in range(planes):
        low, high = halos(up_ref, down_ref, p, half)
        lay(s0, p, low)
        lay(s0, 2 * planes + p, high)
        lay(s0, planes + p, rows_of(own_ref, planes + p, half))
    low, high = halos(up_ref, down_ref, planes, half)
    firsts = [low] + [rows_of(own_ref, p, half) for p in range(planes)] + [high]
    for j, z in enumerate(convs(s0, planes - 1, planes + 2, f_ref)):
        y = (firsts[j].astype(F32) + z * sigmoid(z)).astype(BF16)
        if j == 0:
            y = keep(has_low, y)
        if j == planes + 1:
            y = keep(has_high, y)
        mid_ref[j * half : (j + 1) * half, :] = y
        lay(s1, j, y)
    for p, z in enumerate(convs(s1, 1, planes, g_ref)):
        y = (rows_of(own_ref, planes + p, half).astype(F32) + z * sigmoid(z)).astype(BF16)
        send_ref[p * half : (p + 1) * half, :] = y


def forward_second(half, planes, mid_ref, own_ref, up_ref, down_ref, f_ref, g_ref, join_ref, out_ref, s0, s1):
    has_low, has_high = slab_place()
    for p in range(planes):
        low, high = halos(up_ref, down_ref, p, half)
        lay(s0, p, low)
        lay(s0, 2 * planes + p, high)
        lay(s0, planes + p, rows_of(own_ref, p, half))
    tops = []
    for j, z in enumerate(convs(s0, planes - 1, planes + 2, f_ref)):
        y = (rows_of(mid_ref, j, half).astype(F32) + z * sigmoid(z)).astype(BF16)
        if j == 0:
            y = keep(has_low, y)
        elif j == planes + 1:
            y = keep(has_high, y)
        else:
            tops.append(y)
        lay(s1, j, y)
    bottoms = []
    for p, z in enumerate(convs(s1, 1, planes, g_ref)):
        bottoms.append((rows_of(own_ref, p, half).astype(F32) + z * sigmoid(z)).astype(BF16))
    join_planes(tops, join_ref[...], out_ref, 0)
    join_planes(bottoms, join_ref[...], out_ref, out_ref.shape[0] // 2)


def turn(z, low_value, grad):
    sig = sigmoid(z)
    second = (low_value.astype(F32) - z * sig).astype(BF16)
    inner = (sig * (1.0 + z * (1.0 - sig)) * grad).astype(BF16)
    return second, inner


def backward_first(
    half, planes, y_ref, g1_ref, g2_ref, yu_ref, yd_ref, gu_ref, gd_ref, wg_ref, wf_ref, tg_ref,
    send_ref, second_ref, low_grad_ref, carry_ref, s0, s1, s2,
):
    has_low, has_high = slab_place()
    for p in range(planes):
        low, high = halos(yu_ref, yd_ref, p, half)
        lay(s0, p, low)
        lay(s0, 2 * planes + p, high)
        lay(s0, planes + p, rows_of(y_ref, p, half))
    low, high = halos(yu_ref, yd_ref, planes, half)
    lowers = [low] + [rows_of(y_ref, planes + p, half) for p in range(planes)] + [high]
    low, high = halos(gu_ref, gd_ref, 0, half)
    grads = [low] + [rows_of(g2_ref, p, half) for p in range(planes)] + [high]
    for j, z in enumerate(convs(s0, planes - 1, planes + 2, wg_ref)):
        second, inner = turn(z, lowers[j], grads[j].astype(F32))
        if j == 0:
            second, inner = keep(has_low, second), keep(has_low, inner)
        if j == planes + 1:
            second, inner = keep(has_high, second), keep(has_high, inner)
        second_ref[j * half : (j + 1) * half, :] = second
        low_grad_ref[j * half : (j + 1) * half, :] = grads[j]
        lay(s1, j, second)
        lay(s2, j, inner)
    for p, (z, term) in enumerate(zip(convs(s1, 1, planes, wf_ref), convs(s2, 1, planes, tg_ref))):
        carry = rows_of(g1_ref, p, half).astype(F32) + term
        first, inner = turn(z, rows_of(y_ref, p, half), carry)
        carry_ref[p * half : (p + 1) * half, :] = carry
        send_ref[p * half : (p + 1) * half, :] = first
        send_ref[(planes + p) * half : (planes + p + 1) * half, :] = inner


def backward_second(
    half, planes, mine_ref, up_ref, down_ref, second_ref, low_grad_ref, carry_ref,
    tf_ref, wg_ref, wf_ref, tg_ref,
    state_ref, inner_ref, low_ref, top_ref, out_up_ref, out_down_ref, s0, s1, s2, s3,
):
    has_low, has_high = slab_place()
    odd = is_odd()
    for p in range(planes):
        low, high = halos(up_ref, down_ref, p, half)
        lay(s0, p, low)
        lay(s0, 2 * planes + p, high)
        lay(s0, planes + p, rows_of(mine_ref, p, half))
        low, high = halos(up_ref, down_ref, planes + p, half)
        lay(s2, p, low)
        lay(s2, 2 * planes + p, high)
        lay(s2, planes + p, rows_of(mine_ref, planes + p, half))
    wide = (planes - 1, planes + 2)
    for j, (term, z) in enumerate(zip(convs(s2, *wide, tf_ref), convs(s0, *wide, wg_ref))):
        grad = rows_of(low_grad_ref, j, half).astype(F32) + term
        second, inner = turn(z, rows_of(second_ref, j, half), grad)
        if j == 0:
            second, inner = keep(has_low, second), keep(has_low, inner)
        elif j == planes + 1:
            second, inner = keep(has_high, second), keep(has_high, inner)
        else:
            low_ref[(j - 1) * half : j * half, :] = grad
            state_ref[(planes + j - 1) * half : (planes + j) * half, :] = second
        lay(s1, j, second)
        lay(s3, j, inner)
    inners = []
    for p, (z, term) in enumerate(zip(convs(s1, 1, planes, wf_ref), convs(s3, 1, planes, tg_ref))):
        carry = rows_of(carry_ref, p, half) + term
        first, inner = turn(z, rows_of(mine_ref, p, half), carry)
        state_ref[p * half : (p + 1) * half, :] = first
        top_ref[p * half : (p + 1) * half, :] = carry.astype(BF16)
        inner_ref[p * half : (p + 1) * half, :] = inner
        inners.append(inner)
    out_up_ref[...] = pick(odd, inners[0], inners[planes - 1])
    out_down_ref[...] = pick(odd, inners[planes - 1], inners[0])


def backward_third(
    half, planes, inner_ref, up_ref, down_ref, low_ref, top_ref, tf_ref, join_ref, fwd_ref, state_ref,
    fwd_hbm, state_hbm, grad_hbm, s0, grad_ref, sems,
):
    fwd_copy = pltpu.make_async_copy(fwd_ref, fwd_hbm, sems.at[0])
    state_copy = pltpu.make_async_copy(state_ref, state_hbm, sems.at[1])
    fwd_copy.start()
    state_copy.start()
    low, high = halos(up_ref, down_ref, 0, half)
    lay(s0, 0, low)
    lay(s0, planes + 1, high)
    for p in range(planes):
        lay(s0, 1 + p, rows_of(inner_ref, p, half))
    middle = grad_ref.shape[0] // 2
    join_planes([rows_of(top_ref, p, half) for p in range(planes)], join_ref[...], grad_ref, 0)
    top_copy = pltpu.make_async_copy(grad_ref.at[:middle], grad_hbm.at[:middle], sems.at[2])
    top_copy.start()
    terms = convs(s0, 1, planes, tf_ref)
    lows = [(rows_of(low_ref, p, half) + term).astype(BF16) for p, term in enumerate(terms)]
    join_planes(lows, join_ref[...], grad_ref, middle)
    low_copy = pltpu.make_async_copy(grad_ref.at[middle:], grad_hbm.at[middle:], sems.at[3])
    low_copy.start()
    fwd_copy.wait()
    state_copy.wait()
    top_copy.wait()
    low_copy.wait()


def pack_state(half, planes, state_ref, join_ref, out_ref):
    for h in range(2):
        values = [rows_of(state_ref, h * planes + p, half) for p in range(planes)]
        join_planes(values, join_ref[...], out_ref, h * out_ref.shape[0] // 2)


def call(body, outs, scratch, flops, *args, far_out=False):
    near, far = pl.BlockSpec(memory_space=pltpu.VMEM), pl.BlockSpec(memory_space=pltpu.HBM)
    return pl.pallas_call(
        body,
        out_shape=[jax.ShapeDtypeStruct(shape, dtype) for shape, dtype in outs],
        in_specs=[near] * len(args),
        out_specs=[far if far_out else near] * len(outs),
        scratch_shapes=[pltpu.VMEM(shape, BF16) if isinstance(shape, tuple) else shape for shape in scratch],
        compiler_params=pltpu.CompilerParams(vmem_limit_bytes=16 << 20),
        cost_estimate=pl.CostEstimate(flops=flops, bytes_accessed=1 << 20, transcendentals=0),
    )(*args)


def raw_view(block):
    chans, planes, cells = block.shape
    tiles = cells // LANES
    return block.reshape(chans, planes, tiles, LANES).transpose(0, 2, 1, 3).reshape(-1, LANES)


def from_raw(raw, chans, planes, cells):
    tiles = cells // LANES
    return raw.reshape(chans, tiles, planes, LANES).transpose(0, 2, 1, 3).reshape(1, chans, planes, cells)


def round_trips(sections, slabs):
    ahead = []
    for s in range(0, sections, 2):
        order = [s * slabs + z for z in range(slabs)] + [(s + 1) * slabs + z for z in reversed(range(slabs))]
        ahead += list(zip(order, order[1:] + order[:1]))
    return ahead, [(b, a) for a, b in ahead]


def shards(fwd_states, back_states, back_grads, batch_in, head_state, head_grad, couplings):
    sections, slabs = lax.axis_size("section"), lax.axis_size("slab")
    ahead, behind = round_trips(sections, slabs)
    _, chans, planes, cells = fwd_states.shape
    half = chans // 2

    def swap(up, down):
        from_up = lax.ppermute(up, ("section", "slab"), ahead)
        from_down = lax.ppermute(down, ("section", "slab"), behind)
        return from_up, from_down

    def along(value, step):
        return lax.ppermute(value, "section", [(s, (s + step) % sections) for s in range(sections)])

    got_y = along(raw_view(back_states[0]), -1)
    grads = raw_view(back_grads[0])
    middle = grads.shape[0] // 2
    grads_low, grads_high = grads[middle:], grads[:middle]
    got_g2 = along(grads_low, -1)
    got_g1 = along(grads_high, -1)
    source, got_y = lax.optimization_barrier((raw_view(fwd_states[0]), got_y))
    got_x = along(source, 1)

    def planes_of(count, dtype=BF16):
        return ((count * half, cells), dtype)

    unit = 2 * 9 * half * 3 * half * cells
    raw_shape = ((chans * planes * cells // LANES, LANES), BF16)
    *weights, split, join = call(
        functools.partial(prepare, planes, cells),
        [((6 * half, 12 * half), BF16)] * (4 * PAIRS) + [((256, 256), BF16)] * 2, [], 40 * unit, couplings,
    )
    direct, turned = weights[: 2 * PAIRS], weights[2 * PAIRS :]

    sizes = (half, planes, cells)
    y_own, y_up, y_down = call(
        functools.partial(unpack_state, True, 0, *sizes),
        [planes_of(2 * planes), planes_of(planes + 1), planes_of(planes + 1)], [], unit, got_y, raw_view(head_state), split,
    )
    g2_own, g_up, g_down = call(
        functools.partial(unpack_grad, 1, *sizes),
        [planes_of(planes), planes_of(1), planes_of(1)], [], unit, got_g2, raw_view(head_grad), split,
    )
    (g1_own,) = call(
        functools.partial(unpack_grad, 0, *sizes), [planes_of(planes)], [], unit,
        got_g1, raw_view(head_grad), split,
    )
    x_own, x_up, x_down = call(
        functools.partial(unpack_state, False, 1, *sizes),
        [planes_of(2 * planes), planes_of(planes + 1), planes_of(planes + 1)], [], unit, got_x, raw_view(batch_in), split,
    )
    yu, yd = swap(y_up, y_down)
    gu, gd = swap(g_up, g_down)
    xu, xd = swap(x_up, x_down)

    wide = ((3 * planes) * 3 * half, cells)
    near = ((planes + 2) * 3 * half, cells)
    send, second, low_grad, carry = call(
        functools.partial(backward_first, half, planes),
        [planes_of(2 * planes), planes_of(planes + 2), planes_of(planes + 2), planes_of(planes, F32)],
        [wide, near, near], 8 * unit,
        y_own, g1_own, g2_own, yu, yd, gu, gd, direct[3], direct[2], turned[3],
    )
    su, sd = swap(send, send)
    mid, low_own = call(
        functools.partial(forward_first, half, planes),
        [planes_of(planes + 2), planes_of(planes)], [wide, near], 6 * unit,
        x_own, xu, xd, direct[0], direct[1],
    )
    fu, fd = swap(low_own, low_own)
    state, inner, low, top, iu, id_ = call(
        functools.partial(backward_second, half, planes),
        [planes_of(2 * planes), planes_of(planes), planes_of(planes, F32), planes_of(planes), planes_of(1), planes_of(1)],
        [wide, near, wide, near], 12 * unit,
        send, su, sd, second, low_grad, carry, turned[2], direct[1], direct[0], turned[1],
    )
    iu, id_ = swap(iu, id_)
    (fwd_raw,) = call(
        functools.partial(forward_second, half, planes), [raw_shape], [wide, near], 6 * unit,
        mid, low_own, fu, fd, direct[2], direct[3], join,
    )
    (state_raw,) = call(functools.partial(pack_state, half, planes), [raw_shape], [], unit, state, join)
    fwd_raw, state_raw, grad_raw = call(
        functools.partial(backward_third, half, planes), [raw_shape] * 3,
        [near, raw_shape[0], pltpu.SemaphoreType.DMA((4,))], 2 * unit,
        inner, iu, id_, low, top, turned[0], join, fwd_raw, state_raw, far_out=True,
    )
    shape = (chans, planes, cells)
    return from_raw(fwd_raw, *shape), from_raw(state_raw, *shape), from_raw(grad_raw, *shape)


def solution(mesh):
    return jax.shard_map(
        shards,
        mesh=mesh,
        in_specs=(
            P("section", None, "slab", None),
            P("section", None, "slab", None),
            P("section", None, "slab", None),
            P(None, "slab", None),
            P(None, "slab", None),
            P(None, "slab", None),
            P("section", None, None, None, None),
        ),
        out_specs=(
            P("section", None, "slab", None),
            P("section", None, "slab", None),
            P("section", None, "slab", None),
        ),
        check_vma=False,
    )
```

```python
import functools

import jax
import jax.numpy as jnp
from jax import lax
from jax.experimental import pallas as pl
from jax.experimental.pallas import tpu as pltpu
from jax.sharding import PartitionSpec as P


WID = 32
PAIRS = 2
LANES = 128
F32 = jnp.float32
BF16 = jnp.bfloat16


def dot(a, b):
    return jnp.dot(a, b, preferred_element_type=F32)


def slab_place():
    z = lax.axis_index("slab")
    return z > 0, z < lax.axis_size("slab") - 1


def is_odd():
    return lax.rem(lax.axis_index("section"), 2) == 1


def pick(flag, yes, no):
    return jnp.where(jnp.full(no.shape, flag), yes, no)


def keep(flag, value):
    return jnp.where(jnp.full(value.shape, flag), value, jnp.zeros((), value.dtype))


def matrices(planes, cells, split_ref, join_ref):
    tiles, chans = chunk_sizes(planes, cells)
    split_ref[...] = shuffle(tiles, planes, chans, False)
    join_ref[...] = shuffle(tiles, planes, chans, True)


def prepare(kernels_ref, split_ref, *out_refs):
    count = 2 * PAIRS
    taps, half = kernels_ref.shape[2], kernels_ref.shape[3]
    row = lax.broadcasted_iota(jnp.int32, (half, half), 0)
    col = lax.broadcasted_iota(jnp.int32, (half, half), 1)
    unit = jnp.where(row == col, 1.0, 0.0).astype(BF16)
    for q in range(count):
        mine = [kernels_ref[0, q, k] for k in range(taps)]
        turned = [
            lax.dot_general(unit, m, (((1,), (1,)), ((), ())), preferred_element_type=F32).astype(BF16)
            for m in mine
        ]
        for b in range(3):
            pieces = [mine[9 * a + 3 * b + c] for a in range(3) for c in range(3)]
            out_refs[q][b * half : (b + 1) * half, :] = jnp.concatenate(pieces, axis=1)
            pieces = [turned[26 - (9 * a + 3 * b + c)] for a in range(3) for c in range(3)]
            out_refs[count + q][b * half : (b + 1) * half, :] = jnp.concatenate(pieces, axis=1)


def shuffle(tiles, planes, chans, back):
    size = tiles * planes * chans
    row = lax.broadcasted_iota(jnp.int32, (size, size), 1 if back else 0)
    col = lax.broadcasted_iota(jnp.int32, (size, size), 0 if back else 1)
    tp, c = row // chans, row % chans
    tile, plane = tp // planes, tp % planes
    return jnp.where(col == c * (tiles * planes) + tile * planes + plane, 1.0, 0.0).astype(BF16)


def chunk_sizes(planes, cells):
    tiles = cells // LANES
    return tiles, 256 // (tiles * planes)


def split_planes(raw, matrix, half, planes, cells):
    tiles, chans = chunk_sizes(planes, cells)
    rows = tiles * planes * chans
    chunks = raw.shape[0] // rows
    parts = {}
    for g in range(0, chunks, 2):
        both = jnp.concatenate([raw[g * rows : (g + 1) * rows], raw[(g + 1) * rows : (g + 2) * rows]], axis=1)
        got = dot(matrix, both).astype(BF16)
        for i in range(2):
            for p in range(planes):
                pieces = [
                    got[(t * planes + p) * chans : (t * planes + p + 1) * chans, i * LANES : (i + 1) * LANES]
                    for t in range(tiles)
                ]
                parts[g + i, p] = jnp.concatenate(pieces, axis=1)
    per = half // chans
    count = chunks // per
    return [
        [jnp.concatenate([parts[h * per + j, p] for j in range(per)], axis=0) for p in range(planes)]
        for h in range(count)
    ]


def join_planes(values, matrix, out_ref, base):
    planes, (half, cells) = len(values), values[0].shape
    tiles, chans = chunk_sizes(planes, cells)
    rows = tiles * planes * chans
    for g in range(0, half // chans, 2):
        sides = []
        for i in range(2):
            lines = slice((g + i) * chans, (g + i + 1) * chans)
            sides.append(
                jnp.concatenate(
                    [
                        values[p][lines, t * LANES : (t + 1) * LANES]
                        for t in range(tiles)
                        for p in range(planes)
                    ],
                    axis=0,
                )
            )
        got = dot(matrix, jnp.concatenate(sides, axis=1)).astype(BF16)
        for i in range(2):
            start = base + (g + i) * rows
            out_ref[start : start + rows, :] = got[:, i * LANES : (i + 1) * LANES]


def lay(stack_ref, slot, plane):
    half, cells = plane.shape
    base = slot * 3 * half
    wide = plane.astype(F32)
    column = lax.broadcasted_iota(jnp.int32, wide.shape, 1) % WID
    left = jnp.where(column > 0, pltpu.roll(wide, 1, 1), 0.0)
    right = jnp.where(column < WID - 1, pltpu.roll(wide, cells - 1, 1), 0.0)
    stack_ref[base : base + half, :] = left.astype(BF16)
    stack_ref[base + half : base + 2 * half, :] = plane.astype(BF16)
    stack_ref[base + 2 * half : base + 3 * half, :] = right.astype(BF16)


def conv(stack_ref, slot, weight_ref):
    half = weight_ref.shape[0] // 3
    cells = stack_ref.shape[1]
    begin = (slot - 1) * 3 * half
    total = dot(weight_ref[...], stack_ref[begin : begin + 9 * half, :])
    cell = lax.broadcasted_iota(jnp.int32, (half, cells), 1)
    above = jnp.where(cell >= WID, pltpu.roll(total[:half], WID, 1), 0.0)
    below = jnp.where(cell < cells - WID, pltpu.roll(total[2 * half :], cells - WID, 1), 0.0)
    return above + total[half : 2 * half] + below


def sigmoid(z):
    return jax.nn.sigmoid(z)


def rows_of(ref, index, half):
    return ref[index * half : (index + 1) * half, :]


def unpack_state(edge, wide_half, half, planes, cells, got_ref, edge_ref, matrix_ref, own_ref, up_ref, down_ref):
    at = lax.axis_index("section")
    last = lax.axis_size("section") - 1
    at_edge = at == (last if edge else 0)
    raw = pick(at_edge, edge_ref[...], got_ref[...])
    parts = split_planes(raw, matrix_ref[...], half, planes, cells)
    for h in range(2):
        for p in range(planes):
            own_ref[(h * planes + p) * half : (h * planes + p + 1) * half, :] = parts[h][p]
    other = parts[1 - wide_half]
    odd = is_odd()
    base = 0
    if wide_half is not None:
        for p in range(planes):
            up_ref[p * half : (p + 1) * half, :] = parts[wide_half][p]
            down_ref[p * half : (p + 1) * half, :] = parts[wide_half][p]
        base = planes * half
    up_ref[base : base + half, :] = pick(odd, other[0], other[planes - 1])
    down_ref[base : base + half, :] = pick(odd, other[planes - 1], other[0])


def unpack_grad(part, half, planes, cells, got_ref, edge_ref, matrix_ref, own_ref, *send_refs):
    at_edge = lax.axis_index("section") == lax.axis_size("section") - 1
    rows = got_ref.shape[0]
    raw = pick(at_edge, edge_ref[part * rows : (part + 1) * rows, :], got_ref[...])
    (parts,) = split_planes(raw, matrix_ref[...], half, planes, cells)
    for p in range(planes):
        own_ref[p * half : (p + 1) * half, :] = parts[p]
    if send_refs:
        up_ref, down_ref = send_refs
        odd = is_odd()
        up_ref[...] = pick(odd, parts[0], parts[planes - 1])
        down_ref[...] = pick(odd, parts[planes - 1], parts[0])


def halos(up_ref, down_ref, index, half):
    has_low, has_high = slab_place()
    odd = is_odd()
    first, second = rows_of(up_ref, index, half), rows_of(down_ref, index, half)
    low = keep(has_low, pick(odd, second, first))
    high = keep(has_high, pick(odd, first, second))
    return low, high


def forward_first(half, planes, own_ref, up_ref, down_ref, f_ref, g_ref, mid_ref, send_ref, s0, s1):
    has_low, has_high = slab_place()
    for p in range(planes):
        low, high = halos(up_ref, down_ref, p, half)
        lay(s0, p, low)
        lay(s0, 2 * planes + p, high)
        lay(s0, planes + p, rows_of(own_ref, planes + p, half))
    low, high = halos(up_ref, down_ref, planes, half)
    firsts = [low] + [rows_of(own_ref, p, half) for p in range(planes)] + [high]
    for j in range(planes + 2):
        z = conv(s0, planes - 1 + j, f_ref)
        y = (firsts[j].astype(F32) + z * sigmoid(z)).astype(BF16)
        if j == 0:
            y = keep(has_low, y)
        if j == planes + 1:
            y = keep(has_high, y)
        mid_ref[j * half : (j + 1) * half, :] = y
        lay(s1, j, y)
    for p in range(planes):
        z = conv(s1, 1 + p, g_ref)
        y = (rows_of(own_ref, planes + p, half).astype(F32) + z * sigmoid(z)).astype(BF16)
        send_ref[p * half : (p + 1) * half, :] = y


def forward_second(half, planes, mid_ref, own_ref, up_ref, down_ref, f_ref, g_ref, join_ref, out_ref, s0, s1):
    has_low, has_high = slab_place()
    for p in range(planes):
        low, high = halos(up_ref, down_ref, p, half)
        lay(s0, p, low)
        lay(s0, 2 * planes + p, high)
        lay(s0, planes + p, rows_of(own_ref, p, half))
    tops = []
    for j in range(planes + 2):
        z = conv(s0, planes - 1 + j, f_ref)
        y = (rows_of(mid_ref, j, half).astype(F32) + z * sigmoid(z)).astype(BF16)
        if j == 0:
            y = keep(has_low, y)
        elif j == planes + 1:
            y = keep(has_high, y)
        else:
            tops.append(y)
        lay(s1, j, y)
    bottoms = []
    for p in range(planes):
        z = conv(s1, 1 + p, g_ref)
        bottoms.append((rows_of(own_ref, p, half).astype(F32) + z * sigmoid(z)).astype(BF16))
    join_planes(tops, join_ref[...], out_ref, 0)
    join_planes(bottoms, join_ref[...], out_ref, out_ref.shape[0] // 2)


def turn(z, low_value, grad):
    sig = sigmoid(z)
    second = (low_value.astype(F32) - z * sig).astype(BF16)
    inner = (sig * (1.0 + z * (1.0 - sig)) * grad).astype(BF16)
    return second, inner


def backward_first(
    half, planes, y_ref, g1_ref, g2_ref, yu_ref, yd_ref, gu_ref, gd_ref, wg_ref, wf_ref, tg_ref,
    send_ref, second_ref, low_grad_ref, carry_ref, s0, s1, s2,
):
    has_low, has_high = slab_place()
    for p in range(planes):
        low, high = halos(yu_ref, yd_ref, p, half)
        lay(s0, p, low)
        lay(s0, 2 * planes + p, high)
        lay(s0, planes + p, rows_of(y_ref, p, half))
    low, high = halos(yu_ref, yd_ref, planes, half)
    lowers = [low] + [rows_of(y_ref, planes + p, half) for p in range(planes)] + [high]
    low, high = halos(gu_ref, gd_ref, 0, half)
    grads = [low] + [rows_of(g2_ref, p, half) for p in range(planes)] + [high]
    for j in range(planes + 2):
        z = conv(s0, planes - 1 + j, wg_ref)
        second, inner = turn(z, lowers[j], grads[j].astype(F32))
        if j == 0:
            second, inner = keep(has_low, second), keep(has_low, inner)
        if j == planes + 1:
            second, inner = keep(has_high, second), keep(has_high, inner)
        second_ref[j * half : (j + 1) * half, :] = second
        low_grad_ref[j * half : (j + 1) * half, :] = grads[j]
        lay(s1, j, second)
        lay(s2, j, inner)
    for p in range(planes):
        z = conv(s1, 1 + p, wf_ref)
        carry = rows_of(g1_ref, p, half).astype(F32) + conv(s2, 1 + p, tg_ref)
        first, inner = turn(z, rows_of(y_ref, p, half), carry)
        carry_ref[p * half : (p + 1) * half, :] = carry
        send_ref[p * half : (p + 1) * half, :] = first
        send_ref[(planes + p) * half : (planes + p + 1) * half, :] = inner


def backward_second(
    half, planes, mine_ref, up_ref, down_ref, second_ref, low_grad_ref, carry_ref,
    tf_ref, wg_ref, wf_ref, tg_ref,
    state_ref, inner_ref, low_ref, top_ref, out_up_ref, out_down_ref, s0, s1, s2, s3,
):
    has_low, has_high = slab_place()
    odd = is_odd()
    for p in range(planes):
        low, high = halos(up_ref, down_ref, p, half)
        lay(s0, p, low)
        lay(s0, 2 * planes + p, high)
        lay(s0, planes + p, rows_of(mine_ref, p, half))
        low, high = halos(up_ref, down_ref, planes + p, half)
        lay(s2, p, low)
        lay(s2, 2 * planes + p, high)
        lay(s2, planes + p, rows_of(mine_ref, planes + p, half))
    for j in range(planes + 2):
        grad = rows_of(low_grad_ref, j, half).astype(F32) + conv(s2, planes - 1 + j, tf_ref)
        z = conv(s0, planes - 1 + j, wg_ref)
        second, inner = turn(z, rows_of(second_ref, j, half), grad)
        if j == 0:
            second, inner = keep(has_low, second), keep(has_low, inner)
        elif j == planes + 1:
            second, inner = keep(has_high, second), keep(has_high, inner)
        else:
            low_ref[(j - 1) * half : j * half, :] = grad
            state_ref[(planes + j - 1) * half : (planes + j) * half, :] = second
        lay(s1, j, second)
        lay(s3, j, inner)
    inners = []
    for p in range(planes):
        z = conv(s1, 1 + p, wf_ref)
        carry = rows_of(carry_ref, p, half) + conv(s3, 1 + p, tg_ref)
        first, inner = turn(z, rows_of(mine_ref, p, half), carry)
        state_ref[p * half : (p + 1) * half, :] = first
        top_ref[p * half : (p + 1) * half, :] = carry.astype(BF16)
        inner_ref[p * half : (p + 1) * half, :] = inner
        inners.append(inner)
    out_up_ref[...] = pick(odd, inners[0], inners[planes - 1])
    out_down_ref[...] = pick(odd, inners[planes - 1], inners[0])


def backward_third(
    half, planes, inner_ref, up_ref, down_ref, low_ref, top_ref, tf_ref, join_ref, fwd_ref, state_ref,
    fwd_hbm, state_hbm, grad_hbm, s0, grad_ref, sems,
):
    fwd_copy = pltpu.make_async_copy(fwd_ref, fwd_hbm, sems.at[0])
    state_copy = pltpu.make_async_copy(state_ref, state_hbm, sems.at[1])
    middle = top_ref.shape[0]
    top_copy = pltpu.make_async_copy(top_ref, grad_hbm.at[:middle], sems.at[2])
    fwd_copy.start()
    state_copy.start()
    top_copy.start()
    low, high = halos(up_ref, down_ref, 0, half)
    lay(s0, 0, low)
    lay(s0, planes + 1, high)
    for p in range(planes):
        lay(s0, 1 + p, rows_of(inner_ref, p, half))
    lows = [(rows_of(low_ref, p, half) + conv(s0, 1 + p, tf_ref)).astype(BF16) for p in range(planes)]
    join_planes(lows, join_ref[...], grad_ref, 0)
    low_copy = pltpu.make_async_copy(grad_ref, grad_hbm.at[middle:], sems.at[3])
    low_copy.start()
    fwd_copy.wait()
    state_copy.wait()
    top_copy.wait()
    low_copy.wait()


def pack_state(half, planes, state_ref, top_ref, join_ref, out_ref, out_top_ref):
    join_planes([rows_of(top_ref, p, half) for p in range(planes)], join_ref[...], out_top_ref, 0)
    for h in range(2):
        values = [rows_of(state_ref, h * planes + p, half) for p in range(planes)]
        join_planes(values, join_ref[...], out_ref, h * out_ref.shape[0] // 2)


def call(body, outs, scratch, flops, *args, far_out=False):
    near, far = pl.BlockSpec(memory_space=pltpu.VMEM), pl.BlockSpec(memory_space=pltpu.HBM)
    return pl.pallas_call(
        body,
        out_shape=[jax.ShapeDtypeStruct(shape, dtype) for shape, dtype in outs],
        in_specs=[near] * len(args),
        out_specs=[far if far_out else near] * len(outs),
        scratch_shapes=[pltpu.VMEM(shape, BF16) if isinstance(shape, tuple) else shape for shape in scratch],
        compiler_params=pltpu.CompilerParams(vmem_limit_bytes=16 << 20),
        cost_estimate=pl.CostEstimate(flops=flops, bytes_accessed=1 << 20, transcendentals=0),
    )(*args)


def raw_view(block):
    chans, planes, cells = block.shape
    tiles = cells // LANES
    return block.reshape(chans, planes, tiles, LANES).transpose(0, 2, 1, 3).reshape(-1, LANES)


def from_raw(raw, chans, planes, cells):
    tiles = cells // LANES
    return raw.reshape(chans, tiles, planes, LANES).transpose(0, 2, 1, 3).reshape(1, chans, planes, cells)


def round_trips(sections, slabs):
    ahead = []
    for s in range(0, sections, 2):
        order = [s * slabs + z for z in range(slabs)] + [(s + 1) * slabs + z for z in reversed(range(slabs))]
        ahead += list(zip(order, order[1:] + order[:1]))
    return ahead, [(b, a) for a, b in ahead]


def shards(fwd_states, back_states, back_grads, batch_in, head_state, head_grad, couplings):
    sections, slabs = lax.axis_size("section"), lax.axis_size("slab")
    ahead, behind = round_trips(sections, slabs)
    _, chans, planes, cells = fwd_states.shape
    half = chans // 2

    def swap(up, down):
        from_up = lax.ppermute(up, ("section", "slab"), ahead)
        from_down = lax.ppermute(down, ("section", "slab"), behind)
        return from_up, from_down

    def along(value, step):
        return lax.ppermute(value, "section", [(s, (s + step) % sections) for s in range(sections)])

    got_y = along(raw_view(back_states[0]), -1)
    grads = raw_view(back_grads[0])
    middle = grads.shape[0] // 2
    grads_low, grads_high = grads[middle:], grads[:middle]
    got_g2 = along(grads_low, -1)
    got_g1 = along(grads_high, -1)
    source, got_y = lax.optimization_barrier((raw_view(fwd_states[0]), got_y))
    got_x = along(source, 1)

    def planes_of(count, dtype=BF16):
        return ((count * half, cells), dtype)

    unit = 2 * 9 * half * 3 * half * cells
    raw_shape = ((chans * planes * cells // LANES, LANES), BF16)
    split, join = call(functools.partial(matrices, planes, cells), [((256, 256), BF16)] * 2, [], 40 * unit)
    weights = call(prepare, [((3 * half, 9 * half), BF16)] * (4 * PAIRS), [], 40 * unit, couplings, split)
    direct, turned = weights[: 2 * PAIRS], weights[2 * PAIRS :]

    sizes = (half, planes, cells)
    y_own, y_up, y_down = call(
        functools.partial(unpack_state, True, 0, *sizes),
        [planes_of(2 * planes), planes_of(planes + 1), planes_of(planes + 1)], [], unit, got_y, raw_view(head_state), split,
    )
    g2_own, g_up, g_down = call(
        functools.partial(unpack_grad, 1, *sizes),
        [planes_of(planes), planes_of(1), planes_of(1)], [], unit, got_g2, raw_view(head_grad), split,
    )
    (g1_own,) = call(
        functools.partial(unpack_grad, 0, *sizes), [planes_of(planes)], [], unit,
        got_g1, raw_view(head_grad), split,
    )
    x_own, x_up, x_down = call(
        functools.partial(unpack_state, False, 1, *sizes),
        [planes_of(2 * planes), planes_of(planes + 1), planes_of(planes + 1)], [], unit, got_x, raw_view(batch_in), split,
    )
    yu, yd = swap(y_up, y_down)
    gu, gd = swap(g_up, g_down)
    xu, xd = swap(x_up, x_down)

    wide = ((3 * planes) * 3 * half, cells)
    near = ((planes + 2) * 3 * half, cells)
    send, second, low_grad, carry = call(
        functools.partial(backward_first, half, planes),
        [planes_of(2 * planes), planes_of(planes + 2), planes_of(planes + 2), planes_of(planes, F32)],
        [wide, near, near], 8 * unit,
        y_own, g1_own, g2_own, yu, yd, gu, gd, direct[3], direct[2], turned[3],
    )
    su, sd = swap(send, send)
    mid, low_own = call(
        functools.partial(forward_first, half, planes),
        [planes_of(planes + 2), planes_of(planes)], [wide, near], 6 * unit,
        x_own, xu, xd, direct[0], direct[1],
    )
    fu, fd = swap(low_own, low_own)
    state, inner, low, top, iu, id_ = call(
        functools.partial(backward_second, half, planes),
        [planes_of(2 * planes), planes_of(planes), planes_of(planes, F32), planes_of(planes), planes_of(1), planes_of(1)],
        [wide, near, wide, near], 12 * unit,
        send, su, sd, second, low_grad, carry, turned[2], direct[1], direct[0], turned[1],
    )
    iu, id_ = swap(iu, id_)
    (fwd_raw,) = call(
        functools.partial(forward_second, half, planes), [raw_shape], [wide, near], 6 * unit,
        mid, low_own, fu, fd, direct[2], direct[3], join,
    )
    half_raw = ((raw_shape[0][0] // 2, LANES), BF16)
    state_raw, top_raw = call(
        functools.partial(pack_state, half, planes), [raw_shape, half_raw], [], unit, state, top, join
    )
    fwd_raw, state_raw, grad_raw = call(
        functools.partial(backward_third, half, planes), [raw_shape] * 3,
        [near, half_raw[0], pltpu.SemaphoreType.DMA((4,))], 2 * unit,
        inner, iu, id_, low, top_raw, turned[0], join, fwd_raw, state_raw, far_out=True,
    )
    shape = (chans, planes, cells)
    return from_raw(fwd_raw, *shape), from_raw(state_raw, *shape), from_raw(grad_raw, *shape)


def solution(mesh):
    return jax.shard_map(
        shards,
        mesh=mesh,
        in_specs=(
            P("section", None, "slab", None),
            P("section", None, "slab", None),
            P("section", None, "slab", None),
            P(None, "slab", None),
            P(None, "slab", None),
            P(None, "slab", None),
            P("section", None, None, None, None),
        ),
        out_specs=(
            P("section", None, "slab", None),
            P("section", None, "slab", None),
            P("section", None, "slab", None),
        ),
        check_vma=False,
    )
```

```python
import functools

import jax
import jax.numpy as jnp
from jax import lax
from jax.experimental import pallas as pl
from jax.experimental.pallas import tpu as pltpu
from jax.sharding import PartitionSpec as P


WID = 32
PAIRS = 2
LANES = 128
F32 = jnp.float32
BF16 = jnp.bfloat16


def dot(a, b):
    return jnp.dot(a, b, preferred_element_type=F32)


def slab_place():
    z = lax.axis_index("slab")
    return z > 0, z < lax.axis_size("slab") - 1


def is_odd():
    return lax.rem(lax.axis_index("section"), 2) == 1


def pick(flag, yes, no):
    return jnp.where(jnp.full(no.shape, flag), yes, no)


def keep(flag, value):
    return jnp.where(jnp.full(value.shape, flag), value, jnp.zeros((), value.dtype))


def matrices(planes, cells, split_ref, join_ref):
    tiles, chans = chunk_sizes(planes, cells)
    split_ref[...] = shuffle(tiles, planes, chans, False)
    join_ref[...] = shuffle(tiles, planes, chans, True)


def prepare(kernels_ref, split_ref, *out_refs):
    count = 2 * PAIRS
    taps, half = kernels_ref.shape[2], kernels_ref.shape[3]
    row = lax.broadcasted_iota(jnp.int32, (half, half), 0)
    col = lax.broadcasted_iota(jnp.int32, (half, half), 1)
    unit = jnp.where(row == col, 1.0, 0.0).astype(BF16)
    for q in range(count):
        mine = [kernels_ref[0, q, k] for k in range(taps)]
        turned = [
            lax.dot_general(unit, m, (((1,), (1,)), ((), ())), preferred_element_type=F32).astype(BF16)
            for m in mine
        ]
        for b in range(3):
            pieces = [mine[9 * a + 3 * b + c] for a in range(3) for c in range(3)]
            out_refs[q][b * half : (b + 1) * half, :] = jnp.concatenate(pieces, axis=1)
            pieces = [turned[26 - (9 * a + 3 * b + c)] for a in range(3) for c in range(3)]
            out_refs[count + q][b * half : (b + 1) * half, :] = jnp.concatenate(pieces, axis=1)


def shuffle(tiles, planes, chans, back):
    size = tiles * planes * chans
    row = lax.broadcasted_iota(jnp.int32, (size, size), 1 if back else 0)
    col = lax.broadcasted_iota(jnp.int32, (size, size), 0 if back else 1)
    tp, c = row // chans, row % chans
    tile, plane = tp // planes, tp % planes
    return jnp.where(col == c * (tiles * planes) + tile * planes + plane, 1.0, 0.0).astype(BF16)


def chunk_sizes(planes, cells):
    tiles = cells // LANES
    return tiles, 256 // (tiles * planes)


def split_planes(raw, matrix, half, planes, cells):
    tiles, chans = chunk_sizes(planes, cells)
    rows = tiles * planes * chans
    chunks = raw.shape[0] // rows
    parts = {}
    for g in range(0, chunks, 2):
        both = jnp.concatenate([raw[g * rows : (g + 1) * rows], raw[(g + 1) * rows : (g + 2) * rows]], axis=1)
        got = dot(matrix, both).astype(BF16)
        for i in range(2):
            for p in range(planes):
                pieces = [
                    got[(t * planes + p) * chans : (t * planes + p + 1) * chans, i * LANES : (i + 1) * LANES]
                    for t in range(tiles)
                ]
                parts[g + i, p] = jnp.concatenate(pieces, axis=1)
    per = half // chans
    count = chunks // per
    return [
        [jnp.concatenate([parts[h * per + j, p] for j in range(per)], axis=0) for p in range(planes)]
        for h in range(count)
    ]


def join_planes(values, matrix, out_ref, base):
    planes, (half, cells) = len(values), values[0].shape
    tiles, chans = chunk_sizes(planes, cells)
    rows = tiles * planes * chans
    for g in range(0, half // chans, 2):
        sides = []
        for i in range(2):
            lines = slice((g + i) * chans, (g + i + 1) * chans)
            sides.append(
                jnp.concatenate(
                    [
                        values[p][lines, t * LANES : (t + 1) * LANES]
                        for t in range(tiles)
                        for p in range(planes)
                    ],
                    axis=0,
                )
            )
        got = dot(matrix, jnp.concatenate(sides, axis=1)).astype(BF16)
        for i in range(2):
            start = base + (g + i) * rows
            out_ref[start : start + rows, :] = got[:, i * LANES : (i + 1) * LANES]


def lay(stack_ref, slot, plane):
    half, cells = plane.shape
    base = slot * 3 * half
    wide = plane.astype(F32)
    column = lax.broadcasted_iota(jnp.int32, wide.shape, 1) % WID
    left = jnp.where(column > 0, pltpu.roll(wide, 1, 1), 0.0)
    right = jnp.where(column < WID - 1, pltpu.roll(wide, cells - 1, 1), 0.0)
    stack_ref[base : base + half, :] = left.astype(BF16)
    stack_ref[base + half : base + 2 * half, :] = plane.astype(BF16)
    stack_ref[base + 2 * half : base + 3 * half, :] = right.astype(BF16)


def conv(stack_ref, slot, weight_ref):
    half = weight_ref.shape[0] // 3
    cells = stack_ref.shape[1]
    begin = (slot - 1) * 3 * half
    total = dot(weight_ref[...], stack_ref[begin : begin + 9 * half, :])
    cell = lax.broadcasted_iota(jnp.int32, (half, cells), 1)
    above = jnp.where(cell >= WID, pltpu.roll(total[:half], WID, 1), 0.0)
    below = jnp.where(cell < cells - WID, pltpu.roll(total[2 * half :], cells - WID, 1), 0.0)
    return above + total[half : 2 * half] + below


def sigmoid(z):
    return jax.nn.sigmoid(z)


def rows_of(ref, index, half):
    return ref[index * half : (index + 1) * half, :]


def unpack_state(edge, wide_half, half, planes, cells, got_ref, edge_ref, matrix_ref, own_ref, up_ref, down_ref):
    at = lax.axis_index("section")
    last = lax.axis_size("section") - 1
    at_edge = at == (last if edge else 0)
    raw = pick(at_edge, edge_ref[...], got_ref[...])
    parts = split_planes(raw, matrix_ref[...], half, planes, cells)
    for h in range(2):
        for p in range(planes):
            own_ref[(h * planes + p) * half : (h * planes + p + 1) * half, :] = parts[h][p]
    other = parts[1 - wide_half]
    odd = is_odd()
    base = 0
    if wide_half is not None:
        for p in range(planes):
            up_ref[p * half : (p + 1) * half, :] = parts[wide_half][p]
            down_ref[p * half : (p + 1) * half, :] = parts[wide_half][p]
        base = planes * half
    up_ref[base : base + half, :] = pick(odd, other[0], other[planes - 1])
    down_ref[base : base + half, :] = pick(odd, other[planes - 1], other[0])


def unpack_grad(half, planes, cells, got_ref, edge_ref, matrix_ref, own_ref, up_ref, down_ref):
    at_edge = lax.axis_index("section") == lax.axis_size("section") - 1
    raw = pick(at_edge, edge_ref[got_ref.shape[0] :, :], got_ref[...])
    (parts,) = split_planes(raw, matrix_ref[...], half, planes, cells)
    for p in range(planes):
        own_ref[p * half : (p + 1) * half, :] = parts[p]
    odd = is_odd()
    up_ref[...] = pick(odd, parts[0], parts[planes - 1])
    down_ref[...] = pick(odd, parts[planes - 1], parts[0])


def halos(up_ref, down_ref, index, half):
    has_low, has_high = slab_place()
    odd = is_odd()
    first, second = rows_of(up_ref, index, half), rows_of(down_ref, index, half)
    low = keep(has_low, pick(odd, second, first))
    high = keep(has_high, pick(odd, first, second))
    return low, high


def forward_first(half, planes, own_ref, up_ref, down_ref, f_ref, g_ref, mid_ref, send_ref, s0, s1):
    has_low, has_high = slab_place()
    for p in range(planes):
        low, high = halos(up_ref, down_ref, p, half)
        lay(s0, p, low)
        lay(s0, 2 * planes + p, high)
        lay(s0, planes + p, rows_of(own_ref, planes + p, half))
    low, high = halos(up_ref, down_ref, planes, half)
    firsts = [low] + [rows_of(own_ref, p, half) for p in range(planes)] + [high]
    for j in range(planes + 2):
        z = conv(s0, planes - 1 + j, f_ref)
        y = (firsts[j].astype(F32) + z * sigmoid(z)).astype(BF16)
        if j == 0:
            y = keep(has_low, y)
        if j == planes + 1:
            y = keep(has_high, y)
        mid_ref[j * half : (j + 1) * half, :] = y
        lay(s1, j, y)
    for p in range(planes):
        z = conv(s1, 1 + p, g_ref)
        y = (rows_of(own_ref, planes + p, half).astype(F32) + z * sigmoid(z)).astype(BF16)
        send_ref[p * half : (p + 1) * half, :] = y


def forward_second(half, planes, mid_ref, own_ref, up_ref, down_ref, f_ref, g_ref, join_ref, out_ref, s0, s1):
    has_low, has_high = slab_place()
    for p in range(planes):
        low, high = halos(up_ref, down_ref, p, half)
        lay(s0, p, low)
        lay(s0, 2 * planes + p, high)
        lay(s0, planes + p, rows_of(own_ref, p, half))
    tops = []
    for j in range(planes + 2):
        z = conv(s0, planes - 1 + j, f_ref)
        y = (rows_of(mid_ref, j, half).astype(F32) + z * sigmoid(z)).astype(BF16)
        if j == 0:
            y = keep(has_low, y)
        elif j == planes + 1:
            y = keep(has_high, y)
        else:
            tops.append(y)
        lay(s1, j, y)
    bottoms = []
    for p in range(planes):
        z = conv(s1, 1 + p, g_ref)
        bottoms.append((rows_of(own_ref, p, half).astype(F32) + z * sigmoid(z)).astype(BF16))
    join_planes(tops, join_ref[...], out_ref, 0)
    join_planes(bottoms, join_ref[...], out_ref, out_ref.shape[0] // 2)


def turn(z, low_value, grad):
    sig = sigmoid(z)
    second = (low_value.astype(F32) - z * sig).astype(BF16)
    inner = (sig * (1.0 + z * (1.0 - sig)) * grad).astype(BF16)
    return second, inner


def backward_first(
    half, planes, y_ref, g2_ref, yu_ref, yd_ref, gu_ref, gd_ref, wg_ref, wf_ref, tg_ref,
    first_ref, slope_ref, term_ref, second_ref, low_grad_ref, s0, s1, s2,
):
    has_low, has_high = slab_place()
    for p in range(planes):
        low, high = halos(yu_ref, yd_ref, p, half)
        lay(s0, p, low)
        lay(s0, 2 * planes + p, high)
        lay(s0, planes + p, rows_of(y_ref, p, half))
    low, high = halos(yu_ref, yd_ref, planes, half)
    lowers = [low] + [rows_of(y_ref, planes + p, half) for p in range(planes)] + [high]
    low, high = halos(gu_ref, gd_ref, 0, half)
    grads = [low] + [rows_of(g2_ref, p, half) for p in range(planes)] + [high]
    for j in range(planes + 2):
        z = conv(s0, planes - 1 + j, wg_ref)
        second, inner = turn(z, lowers[j], grads[j].astype(F32))
        if j == 0:
            second, inner = keep(has_low, second), keep(has_low, inner)
        if j == planes + 1:
            second, inner = keep(has_high, second), keep(has_high, inner)
        second_ref[j * half : (j + 1) * half, :] = second
        low_grad_ref[j * half : (j + 1) * half, :] = grads[j]
        lay(s1, j, second)
        lay(s2, j, inner)
    for p in range(planes):
        z = conv(s1, 1 + p, wf_ref)
        term_ref[p * half : (p + 1) * half, :] = conv(s2, 1 + p, tg_ref)
        sig = sigmoid(z)
        first = (rows_of(y_ref, p, half).astype(F32) - z * sig).astype(BF16)
        first_ref[p * half : (p + 1) * half, :] = first
        slope_ref[p * half : (p + 1) * half, :] = sig * (1.0 + z * (1.0 - sig))


def backward_carry(
    half, planes, cells, got_ref, edge_ref, matrix_ref, first_ref, slope_ref, term_ref, send_ref, carry_ref
):
    at_edge = lax.axis_index("section") == lax.axis_size("section") - 1
    raw = pick(at_edge, edge_ref[: got_ref.shape[0], :], got_ref[...])
    (grads,) = split_planes(raw, matrix_ref[...], half, planes, cells)
    for p in range(planes):
        carry = grads[p].astype(F32) + rows_of(term_ref, p, half)
        carry_ref[p * half : (p + 1) * half, :] = carry
        send_ref[p * half : (p + 1) * half, :] = rows_of(first_ref, p, half)
        inner = (rows_of(slope_ref, p, half) * carry).astype(BF16)
        send_ref[(planes + p) * half : (planes + p + 1) * half, :] = inner


def backward_second(
    half, planes, mine_ref, up_ref, down_ref, second_ref, low_grad_ref, carry_ref,
    tf_ref, wg_ref, wf_ref, tg_ref,
    state_ref, inner_ref, low_ref, top_ref, out_up_ref, out_down_ref, s0, s1, s2, s3,
):
    has_low, has_high = slab_place()
    odd = is_odd()
    for p in range(planes):
        low, high = halos(up_ref, down_ref, p, half)
        lay(s0, p, low)
        lay(s0, 2 * planes + p, high)
        lay(s0, planes + p, rows_of(mine_ref, p, half))
        low, high = halos(up_ref, down_ref, planes + p, half)
        lay(s2, p, low)
        lay(s2, 2 * planes + p, high)
        lay(s2, planes + p, rows_of(mine_ref, planes + p, half))
    for j in range(planes + 2):
        grad = rows_of(low_grad_ref, j, half).astype(F32) + conv(s2, planes - 1 + j, tf_ref)
        z = conv(s0, planes - 1 + j, wg_ref)
        second, inner = turn(z, rows_of(second_ref, j, half), grad)
        if j == 0:
            second, inner = keep(has_low, second), keep(has_low, inner)
        elif j == planes + 1:
            second, inner = keep(has_high, second), keep(has_high, inner)
        else:
            low_ref[(j - 1) * half : j * half, :] = grad
            state_ref[(planes + j - 1) * half : (planes + j) * half, :] = second
        lay(s1, j, second)
        lay(s3, j, inner)
    inners = []
    for p in range(planes):
        z = conv(s1, 1 + p, wf_ref)
        carry = rows_of(carry_ref, p, half) + conv(s3, 1 + p, tg_ref)
        first, inner = turn(z, rows_of(mine_ref, p, half), carry)
        state_ref[p * half : (p + 1) * half, :] = first
        top_ref[p * half : (p + 1) * half, :] = carry.astype(BF16)
        inner_ref[p * half : (p + 1) * half, :] = inner
        inners.append(inner)
    out_up_ref[...] = pick(odd, inners[0], inners[planes - 1])
    out_down_ref[...] = pick(odd, inners[planes - 1], inners[0])


def backward_third(
    half, planes, inner_ref, up_ref, down_ref, low_ref, top_ref, tf_ref, join_ref, fwd_ref, state_ref,
    fwd_hbm, state_hbm, grad_hbm, s0, grad_ref, sems,
):
    fwd_copy = pltpu.make_async_copy(fwd_ref, fwd_hbm, sems.at[0])
    state_copy = pltpu.make_async_copy(state_ref, state_hbm, sems.at[1])
    middle = top_ref.shape[0]
    top_copy = pltpu.make_async_copy(top_ref, grad_hbm.at[:middle], sems.at[2])
    fwd_copy.start()
    state_copy.start()
    top_copy.start()
    low, high = halos(up_ref, down_ref, 0, half)
    lay(s0, 0, low)
    lay(s0, planes + 1, high)
    for p in range(planes):
        lay(s0, 1 + p, rows_of(inner_ref, p, half))
    lows = [(rows_of(low_ref, p, half) + conv(s0, 1 + p, tf_ref)).astype(BF16) for p in range(planes)]
    join_planes(lows, join_ref[...], grad_ref, 0)
    low_copy = pltpu.make_async_copy(grad_ref, grad_hbm.at[middle:], sems.at[3])
    low_copy.start()
    fwd_copy.wait()
    state_copy.wait()
    top_copy.wait()
    low_copy.wait()


def pack_state(half, planes, state_ref, top_ref, join_ref, out_ref, out_top_ref):
    join_planes([rows_of(top_ref, p, half) for p in range(planes)], join_ref[...], out_top_ref, 0)
    for h in range(2):
        values = [rows_of(state_ref, h * planes + p, half) for p in range(planes)]
        join_planes(values, join_ref[...], out_ref, h * out_ref.shape[0] // 2)


def call(body, outs, scratch, flops, *args, far_out=False):
    near, far = pl.BlockSpec(memory_space=pltpu.VMEM), pl.BlockSpec(memory_space=pltpu.HBM)
    return pl.pallas_call(
        body,
        out_shape=[jax.ShapeDtypeStruct(shape, dtype) for shape, dtype in outs],
        in_specs=[near] * len(args),
        out_specs=[far if far_out else near] * len(outs),
        scratch_shapes=[pltpu.VMEM(shape, BF16) if isinstance(shape, tuple) else shape for shape in scratch],
        compiler_params=pltpu.CompilerParams(vmem_limit_bytes=16 << 20),
        cost_estimate=pl.CostEstimate(flops=flops, bytes_accessed=1 << 20, transcendentals=0),
    )(*args)


def raw_view(block):
    chans, planes, cells = block.shape
    tiles = cells // LANES
    return block.reshape(chans, planes, tiles, LANES).transpose(0, 2, 1, 3).reshape(-1, LANES)


def from_raw(raw, chans, planes, cells):
    tiles = cells // LANES
    return raw.reshape(chans, tiles, planes, LANES).transpose(0, 2, 1, 3).reshape(1, chans, planes, cells)


def round_trips(sections, slabs):
    ahead = []
    for s in range(0, sections, 2):
        order = [s * slabs + z for z in range(slabs)] + [(s + 1) * slabs + z for z in reversed(range(slabs))]
        ahead += list(zip(order, order[1:] + order[:1]))
    return ahead, [(b, a) for a, b in ahead]


def shards(fwd_states, back_states, back_grads, batch_in, head_state, head_grad, couplings):
    sections, slabs = lax.axis_size("section"), lax.axis_size("slab")
    ahead, behind = round_trips(sections, slabs)
    _, chans, planes, cells = fwd_states.shape
    half = chans // 2

    def swap(up, down):
        from_up = lax.ppermute(up, ("section", "slab"), ahead)
        from_down = lax.ppermute(down, ("section", "slab"), behind)
        return from_up, from_down

    def along(value, step):
        return lax.ppermute(value, "section", [(s, (s + step) % sections) for s in range(sections)])

    got_y = along(raw_view(back_states[0]), -1)
    grads = raw_view(back_grads[0])
    middle = grads.shape[0] // 2
    grads_low, grads_high = grads[middle:], grads[:middle]
    got_g2 = along(grads_low, -1)
    got_g1 = along(grads_high, -1)
    source, got_y = lax.optimization_barrier((raw_view(fwd_states[0]), got_y))
    got_x = along(source, 1)

    def planes_of(count, dtype=BF16):
        return ((count * half, cells), dtype)

    unit = 2 * 9 * half * 3 * half * cells
    raw_shape = ((chans * planes * cells // LANES, LANES), BF16)
    split, join = call(functools.partial(matrices, planes, cells), [((256, 256), BF16)] * 2, [], 40 * unit)
    weights = call(prepare, [((3 * half, 9 * half), BF16)] * (4 * PAIRS), [], 40 * unit, couplings, split)
    direct, turned = weights[: 2 * PAIRS], weights[2 * PAIRS :]

    sizes = (half, planes, cells)
    y_own, y_up, y_down = call(
        functools.partial(unpack_state, True, 0, *sizes),
        [planes_of(2 * planes), planes_of(planes + 1), planes_of(planes + 1)], [], unit, got_y, raw_view(head_state), split,
    )
    g2_own, g_up, g_down = call(
        functools.partial(unpack_grad, *sizes),
        [planes_of(planes), planes_of(1), planes_of(1)], [], unit, got_g2, raw_view(head_grad), split,
    )
    x_own, x_up, x_down = call(
        functools.partial(unpack_state, False, 1, *sizes),
        [planes_of(2 * planes), planes_of(planes + 1), planes_of(planes + 1)], [], unit, got_x, raw_view(batch_in), split,
    )
    yu, yd = swap(y_up, y_down)
    gu, gd = swap(g_up, g_down)
    xu, xd = swap(x_up, x_down)

    wide = ((3 * planes) * 3 * half, cells)
    near = ((planes + 2) * 3 * half, cells)
    first, slope, term, second, low_grad = call(
        functools.partial(backward_first, half, planes),
        [planes_of(planes), planes_of(planes, F32), planes_of(planes, F32), planes_of(planes + 2), planes_of(planes + 2)],
        [wide, near, near], 8 * unit,
        y_own, g2_own, yu, yd, gu, gd, direct[3], direct[2], turned[3],
    )
    send, carry = call(
        functools.partial(backward_carry, *sizes), [planes_of(2 * planes), planes_of(planes, F32)], [],
        unit, got_g1, raw_view(head_grad), split, first, slope, term,
    )
    su, sd = swap(send, send)
    mid, low_own = call(
        functools.partial(forward_first, half, planes),
        [planes_of(planes + 2), planes_of(planes)], [wide, near], 6 * unit,
        x_own, xu, xd, direct[0], direct[1],
    )
    fu, fd = swap(low_own, low_own)
    state, inner, low, top, iu, id_ = call(
        functools.partial(backward_second, half, planes),
        [planes_of(2 * planes), planes_of(planes), planes_of(planes, F32), planes_of(planes), planes_of(1), planes_of(1)],
        [wide, near, wide, near], 12 * unit,
        send, su, sd, second, low_grad, carry, turned[2], direct[1], direct[0], turned[1],
    )
    iu, id_ = swap(iu, id_)
    (fwd_raw,) = call(
        functools.partial(forward_second, half, planes), [raw_shape], [wide, near], 6 * unit,
        mid, low_own, fu, fd, direct[2], direct[3], join,
    )
    half_raw = ((raw_shape[0][0] // 2, LANES), BF16)
    state_raw, top_raw = call(
        functools.partial(pack_state, half, planes), [raw_shape, half_raw], [], unit, state, top, join
    )
    fwd_raw, state_raw, grad_raw = call(
        functools.partial(backward_third, half, planes), [raw_shape] * 3,
        [near, half_raw[0], pltpu.SemaphoreType.DMA((4,))], 2 * unit,
        inner, iu, id_, low, top_raw, turned[0], join, fwd_raw, state_raw, far_out=True,
    )
    shape = (chans, planes, cells)
    return from_raw(fwd_raw, *shape), from_raw(state_raw, *shape), from_raw(grad_raw, *shape)


def solution(mesh):
    return jax.shard_map(
        shards,
        mesh=mesh,
        in_specs=(
            P("section", None, "slab", None),
            P("section", None, "slab", None),
            P("section", None, "slab", None),
            P(None, "slab", None),
            P(None, "slab", None),
            P(None, "slab", None),
            P("section", None, None, None, None),
        ),
        out_specs=(
            P("section", None, "slab", None),
            P("section", None, "slab", None),
            P("section", None, "slab", None),
        ),
        check_vma=False,
    )
```
